32 devices in a mesh: tok: 4 (over y, x), blk: 8 (over z, core).
Axes of the slice: x: 2, y: 2, z: 4, core: 2. Of those that a mesh axis runs over, the one named last changes fastest.
Arguments:
- tokens: bfloat16 [512, 8192], P('tok', 'blk'), may hold values from -6 to 6
- w_blocks: bfloat16 [3072, 128, 128], P('blk'), may hold values from -0.15625 to 0.15625
- blk_row: int32 [3072], P('blk'), may hold values from 0 to 63, as said below
- blk_col: int32 [3072], P('blk'), may hold values from 0 to 319, as said below
- blk_count: int32 [8], P('blk'), may hold values from 96 to 384, as said below
- col_owner: int32 [320], replicated, may hold values from 0 to 7, as said below
- cotangent: bfloat16 [512, 40960], P('tok', 'blk'), may hold values from -6 to 6
Outputs:
- activated: bfloat16 [512, 40960], P('tok', 'blk')
- input_grad: bfloat16 [512, 8192], P('tok', 'blk')
- block_grad: bfloat16 [3072, 128, 128], P('blk', 'tok')
The draws below stay inside these ranges and needn't reach their ends.
Inputs may be any that keep to these rules, and one draw needn't show every extreme that they name: Slots from blk_count[o] on are unused; some owner has exactly 384 live slots. `blk_row`: the live slots of one owner name distinct blocks. `blk_col`: every slot names a block column that col_owner gives to the slot's owner. `col_owner`: each owner owns exactly 40 block columns.
All inputs are finite; a program needn't handle non-finite values.
Results may differ from the reference program's by a relative error of at most 0.018.
Values may be sent and summed in bfloat16 or wider, within the bound.
No kernel may reach another device: no remote copies, remote signals or barrier semaphores. Data moves between devices by JAX's collectives and lax.ppermute only.
A program may use at most 128 MiB of HBM per device.

```python
import jax
import jax.numpy as jnp
from jax import lax

D = 8192
HID = 40960
BLOCK = 128
TOK_DEV = 128
TOKENS = 512
RB = 64
CB = 320
CPD = 40
MAXB = 384
N_TOK = 4
N_BLK = 8


def pattern(key):
    base = jax.random.fold_in(key, 7)
    owners = CB // CPD
    shuffle = jax.random.permutation(jax.random.fold_in(base, 1), CB).astype(jnp.int32)
    col_owner = jnp.zeros((CB,), jnp.int32).at[shuffle].set(jnp.arange(CB, dtype=jnp.int32) // CPD)
    counts = jax.random.randint(jax.random.fold_in(base, 2), (owners,), MAXB // 4, MAXB + 1).astype(jnp.int32)
    fullest = jax.random.randint(jax.random.fold_in(base, 3), (), 0, owners)
    counts = jnp.where(jnp.arange(owners) == fullest, MAXB, counts).astype(jnp.int32)
    owned = jnp.sort(shuffle.reshape(owners, CPD), axis=1)
    keys = jax.random.split(jax.random.fold_in(base, 4), owners)
    picks = jax.vmap(lambda k: jax.random.permutation(k, RB * CPD)[:MAXB])(keys).astype(jnp.int32)
    rows = picks // CPD
    local = picks % CPD
    cols = jnp.take_along_axis(owned, local, axis=1)
    return (col_owner, counts, rows.reshape(-1).astype(jnp.int32), cols.reshape(-1).astype(jnp.int32))


def draw_blk_row(key, part):
    return pattern(key)[2]


def draw_blk_col(key, part):
    return pattern(key)[3]


def draw_blk_count(key, part):
    return pattern(key)[1]


def draw_col_owner(key, part):
    return pattern(key)[0]


def levels(stream_key, extent, cuts, smallest, high):
    level, own = 1.0, jax.random.fold_in(stream_key, 6)
    for axis_at, parts in cuts:
        draws = jnp.exp(jax.random.uniform(jax.random.fold_in(own, axis_at), (parts,), jnp.float32, smallest / len(cuts), high / len(cuts)))
        level = level * jnp.repeat(draws, extent[axis_at] // parts).reshape([-1 if axis == axis_at else 1 for axis in range(len(extent))])
    return level


def centred(stream_key, extent, deviation, reach, cuts=(), kind=jnp.bfloat16):
    gain = levels(stream_key, extent, cuts, -0.22, 0.18) if cuts else 1.0
    result = jax.random.normal(stream_key, extent, jnp.float32) * deviation * gain
    return jnp.minimum(jnp.maximum(result, -reach), reach).astype(kind)


def setup_inputs(seed: int = 0) -> dict:
    splits = jax.random.split(jax.random.key(seed), 8)
    tokens = centred(splits[0], (TOKENS, D), 1.0, 6.0, ((0, 4), (1, 8)))
    w_blocks = centred(splits[1], (N_BLK * MAXB, BLOCK, BLOCK), (BLOCK * MAXB // CPD) ** -0.5, 0.15625, ((0, 8),))
    blk_row = draw_blk_row(jax.random.fold_in(splits[7], 71), 0)
    blk_col = draw_blk_col(jax.random.fold_in(splits[7], 71), 0)
    blk_count = draw_blk_count(jax.random.fold_in(splits[7], 71), 0)
    col_owner = draw_col_owner(jax.random.fold_in(splits[7], 71), 0)
    cotangent = centred(splits[6], (TOKENS, HID), 1.0, 6.0, ((0, 4), (1, 8)))
    return dict(tokens=tokens, w_blocks=w_blocks, blk_row=blk_row, blk_col=blk_col, blk_count=blk_count, col_owner=col_owner, cotangent=cotangent)


def silu_parts(hidden):
    gate = jax.nn.sigmoid(hidden)
    return hidden * gate, gate * (1.0 + hidden * (1.0 - gate))


def reference(tokens, w_blocks, blk_row, blk_col, blk_count, col_owner, cotangent):
    owner_ids = jnp.arange(N_BLK, dtype=jnp.int32)
    member = (col_owner[:, None] == owner_ids[None, :]).astype(jnp.int32)
    column_rank = jnp.sum((jnp.cumsum(member, axis=0) - 1) * member, axis=1)
    x_blocks = tokens.reshape(TOKENS, RB, BLOCK)
    cot_owned = cotangent.reshape(TOKENS, N_BLK, CPD * BLOCK).transpose(1, 0, 2)
    items = (w_blocks.reshape(N_BLK, MAXB, BLOCK, BLOCK), blk_row.reshape(N_BLK, MAXB),
             blk_col.reshape(N_BLK, MAXB), blk_count, cot_owned)

    def per_owner(carry, item):
        weights, rows, cols, count, cot = item
        live_slot = jnp.arange(MAXB, dtype=jnp.int32) < count
        local = column_rank[cols]
        slot_place = ((local[:, None] == jnp.arange(CPD, dtype=jnp.int32)[None, :]) & live_slot[:, None]).astype(jnp.float32)
        slot_inputs = x_blocks[:, rows, :].astype(jnp.float32)
        weights32 = weights.astype(jnp.float32)
        products = jnp.einsum('tsk,skn->tsn', slot_inputs, weights32)
        hidden = jnp.einsum('tsn,sc->tcn', products, slot_place).reshape(TOKENS, CPD * BLOCK)
        activated, derivative = silu_parts(hidden)
        hidden_grad = (cot.astype(jnp.float32) * derivative).astype(jnp.bfloat16)
        hidden_grad = lax.optimization_barrier(hidden_grad).astype(jnp.float32)
        slot_grads = jnp.einsum('tcn,sc->tsn', hidden_grad.reshape(TOKENS, CPD, BLOCK), slot_place)
        back_terms = jnp.einsum('tsn,skn->tsk', slot_grads, weights32)
        row_select = (rows[:, None] == jnp.arange(RB, dtype=jnp.int32)[None, :]).astype(jnp.float32)
        term = jnp.einsum('tsk,sr->trk', back_terms, row_select).reshape(TOKENS, D)
        term = lax.optimization_barrier(term.astype(jnp.bfloat16)).astype(jnp.float32)
        grad_part = jnp.einsum('gtsk,gtsn->gskn', slot_inputs.reshape(N_TOK, TOK_DEV, MAXB, BLOCK),
                               slot_grads.reshape(N_TOK, TOK_DEV, MAXB, BLOCK))
        grad_part = lax.optimization_barrier(grad_part.astype(jnp.bfloat16)).astype(jnp.float32)
        block_grad = jnp.sum(grad_part, axis=0).astype(jnp.bfloat16)
        return carry + term, (activated.astype(jnp.bfloat16), block_grad)

    total, (acts, grads) = lax.scan(per_owner, jnp.zeros((TOKENS, D), jnp.float32), items)
    activated = acts.transpose(1, 0, 2).reshape(TOKENS, HID)
    return activated, total.astype(jnp.bfloat16), grads.reshape(N_BLK * MAXB, BLOCK, BLOCK)
```

```python
import functools

import jax
import jax.numpy as jnp
from jax import lax
from jax.experimental import pallas as pl
from jax.experimental.pallas import tpu as pltpu
from jax.sharding import PartitionSpec as P


GROUP = 4
LIMIT = 34 * 1024 * 1024
VMEM = pl.BlockSpec(memory_space=pltpu.VMEM)
SMEM = pl.BlockSpec(memory_space=pltpu.SMEM)
ANY = pl.BlockSpec(memory_space=pl.ANY)


def group_table(key, other, live, n_keys, pad_other):
    slots = key.shape[0]
    ids = jnp.arange(slots, dtype=jnp.int32)
    keys = jnp.arange(n_keys, dtype=jnp.int32)
    same = (key[:, None] == key[None, :]) & (ids[None, :] < ids[:, None]) & live[None, :]
    rank = jnp.sum(same.astype(jnp.int32), axis=1)
    hit = (key[:, None] == keys[None, :]) & live[:, None]
    groups = (jnp.sum(hit.astype(jnp.int32), axis=0) + GROUP - 1) // GROUP
    start = jnp.sum(jnp.where(keys[None, :] < key[:, None], groups[None, :], 0), axis=1)
    total = (slots + n_keys * (GROUP - 1) + GROUP - 1) // GROUP * GROUP
    place = jnp.where(live, start * GROUP + rank, total)
    pad = slots | (pad_other << 9)
    entry = ids | (other << 9) | (key << 16)
    at = jnp.arange(total, dtype=jnp.int32)
    table = pad + jnp.sum(
        jnp.where(place[None, :] == at[:, None], (entry - pad)[None, :], 0), axis=1
    )
    return table, groups


def each(lo, hi, body, unroll):
    n = hi - lo
    main = n // unroll

    def many(i, carry):
        for u in range(unroll):
            body(lo + i * unroll + u)
        return carry

    def one(i, carry):
        body(i)
        return carry

    lax.fori_loop(0, main, many, 0)
    lax.fori_loop(lo + main * unroll, hi, one, 0)


def unpack(tab, g):
    entries = [tab[g * GROUP + i] for i in range(GROUP)]
    return (
        [e & 511 for e in entries],
        [lax.shift_right_logical(e, 9) & 127 for e in entries],
        lax.shift_right_logical(entries[0], 16),
    )


def lanes(ref, at, i, block):
    return ref[at, :, pl.ds(pl.multiple_of(i * block, block), block)]


def forward_kernel(shards, cuts, tab, meta, *refs):
    x_in = refs[:shards]
    w_ref, cot_ref, act_ref = refs[shards : shards + 3]
    h_refs = refs[shards + 3 : -3]
    x_ref, acc, sem = refs[-3:]
    slots, block, _ = w_ref.shape
    per = x_ref.shape[2] // block
    cols = acc.shape[0]
    copies = []
    for i, ref in enumerate(x_in):
        n = ref.shape[0]
        copies.append(pltpu.make_async_copy(ref, x_ref.at[pl.ds(meta[2 + i], n)], sem.at[i]))
    for copy in copies:
        copy.start()
    acc[...] = jnp.zeros_like(acc)
    x_ref[x_ref.shape[0] - 1, :, 0:block] = jnp.zeros((x_ref.shape[1], block), x_ref.dtype)
    for copy in copies:
        copy.wait()

    def group(g):
        ids, rows, col = unpack(tab, g)
        x = jnp.concatenate([lanes(x_ref, r // per, r % per, block) for r in rows], axis=1)
        w = jnp.concatenate([w_ref[jnp.minimum(s, slots - 1)] for s in ids], axis=0)
        acc[col] += jnp.dot(x, w, preferred_element_type=jnp.float32)

    each(0, meta[0], group, 4)
    for c in range(cols):
        at = slice(c * block, (c + 1) * block)
        hidden = acc[c]
        gate = jax.nn.sigmoid(hidden)
        act_ref[:, at] = (hidden * gate).astype(act_ref.dtype)
        slope = gate * (1.0 + hidden * (1.0 - gate))
        grad = (cot_ref[:, at].astype(jnp.float32) * slope).astype(act_ref.dtype)
        k = max(i for i in range(len(cuts)) if cuts[i] <= c)
        h_refs[k][:, (c - cuts[k]) * block : (c - cuts[k] + 1) * block] = grad


def term_kernel(chunks, tab, meta, *refs):
    h_in = refs[:chunks]
    w_ref = refs[chunks]
    outs = refs[chunks + 1 : -2]
    h_ref, acc = refs[-2:]
    slots, block, _ = w_ref.shape
    acc[...] = jnp.zeros_like(acc)
    at = 0
    for ref in h_in:
        h_ref[:, at : at + ref.shape[1]] = ref[...]
        at += ref.shape[1]
    h_ref[:, at : at + block] = jnp.zeros((h_ref.shape[0], block), h_ref.dtype)

    def group(g):
        ids, cols, row = unpack(tab, g)
        h = jnp.concatenate(
            [h_ref[:, pl.ds(pl.multiple_of(c * block, block), block)] for c in cols], axis=1
        )
        w = jnp.concatenate([w_ref[jnp.minimum(s, slots - 1)] for s in ids], axis=1)
        acc[row] += lax.dot_general(
            h, w, (((1,), (1,)), ((), ())), preferred_element_type=jnp.float32
        )

    each(0, meta[0], group, 4)
    role = 0
    for ref in outs:
        for i in range(ref.shape[0]):
            panel = meta[2 + role]
            per = ref.shape[2] // block
            for j in range(per):
                ref[i, :, j * block : (j + 1) * block] = acc[panel * per + j].astype(ref.dtype)
            role += 1


def grad_kernel(lo_at, shards, base_col, tab, meta, *refs):
    x_in = refs[:shards]
    h_in = refs[shards : -3]
    out_ref, x_ref, sem = refs[-3:]
    if lo_at is not None:
        h_in, old_ref = h_in[:-1], h_in[-1]
    rows_tok, _ = h_in[0].shape[-2:]
    block = out_ref.shape[2]
    part = out_ref.shape[1]
    copies = []
    for i, ref in enumerate(x_in):
        n = ref.shape[0]
        copies.append(pltpu.make_async_copy(ref, x_ref.at[pl.ds(meta[2 + i], n)], sem.at[i]))
    for copy in copies:
        copy.start()
    if lo_at is None:
        out_ref[...] = jnp.zeros_like(out_ref)
    else:
        out_ref[...] = old_ref[...]
    for copy in copies:
        copy.wait()

    def group(g):
        ids, rows, col = unpack(tab, g)
        first = ids[0]
        live = [s < out_ref.shape[0] for s in ids]
        ids = [jnp.where(l, s, first) for l, s in zip(live, ids)]
        rows = [jnp.where(l, r, rows[0]) for l, r in zip(live, rows)]
        x = jnp.concatenate([x_ref[r] for r in rows], axis=0)
        h = []
        for ref in h_in:
            at = pl.ds(pl.multiple_of((col - base_col) * block, block), block)
            if len(ref.shape) == 2:
                h.append(ref[:, at])
            else:
                h += [ref[i, :, at] for i in range(ref.shape[0])]
        h = jnp.concatenate(h, axis=0)
        out = jnp.dot(x, h, preferred_element_type=jnp.float32).astype(out_ref.dtype)
        for i, s in enumerate(ids):
            out_ref[s] = out[i * part : (i + 1) * part]

    each(meta[0], meta[1], group, 4)


def quarter_kernel(me, tok_ref, *refs):
    outs, scratch = refs[:-1], refs[-1]
    block = scratch.shape[1]
    part = outs[0].shape[1]
    for r in range(scratch.shape[0]):
        scratch[r] = tok_ref[:, r * block : (r + 1) * block].T
    for j, ref in enumerate(outs):
        at = pl.multiple_of((me[0] ^ j) * part, part)
        ref[...] = scratch[:, pl.ds(at, part), :]


def along_z(pairs):
    return [(a * 2 + c, b * 2 + c) for a, b in pairs for c in range(2)]


EVEN = along_z([(0, 1), (1, 0), (2, 3), (3, 2)])
ODD = along_z([(1, 2), (2, 1)])
OUTWARD = along_z([(1, 0), (2, 3)])
INWARD = along_z([(0, 1), (3, 2)])
CORES = [(b, b ^ 1) for b in range(8)]
TOK_X = [(t, t ^ 1) for t in range(4)]
TOK_Y = [(t, t ^ 2) for t in range(4)]
TOK_XY = [(t, t ^ 3) for t in range(4)]


def blk(x, pairs):
    return lax.ppermute(x, "blk", pairs)


def tok(x, pairs):
    return lax.ppermute(x, "tok", pairs)


def gather_line(x, middle):
    e1, o1 = blk(x, EVEN), blk(x, ODD)
    p0 = blk(x, CORES)
    o2, e2 = blk(e1, ODD), blk(o1, OUTWARD)
    p1 = blk(e1, CORES)
    e3 = blk(o2, OUTWARD)
    n2 = jnp.where(middle, o1, e2)
    p2 = blk(n2, CORES)
    n3 = jnp.where(middle, o2, e3)
    p3 = blk(n3, CORES)
    return [x, e1, n2, n3, p0, p1, p2, p3]


def on_device(n_tok, n_blk, tokens, w_blocks, blk_row, blk_col, blk_count, col_owner, cotangent):
    fast = (n_tok, n_blk) == (4, 8)
    rows_tok, width = tokens.shape
    slots, block, _ = w_blocks.shape
    cols = cotangent.shape[1] // block
    per = width // block
    n_rows = per * n_blk
    part = block // n_tok
    me_blk = lax.axis_index("blk")
    me_tok = lax.axis_index("tok")
    z, core = me_blk // 2, me_blk % 2
    middle = (z == 1) | (z == 2)
    bf16 = tokens.dtype
    params = pltpu.CompilerParams(vmem_limit_bytes=LIMIT)

    if fast:
        far = [z, z ^ 1, jnp.where(z < 2, 2, 1), jnp.where(z < 2, 3, 0)]
        panels = [f * 2 + core for f in far] + [f * 2 + 1 - core for f in far]
        shards = gather_line(tokens, middle)
        shards = [s[None] for s in shards]
    else:
        panels = [jnp.int32(0)]
        shards = [lax.all_gather(tokens, "blk", axis=0)]

    mine = (col_owner == me_blk)[None, :]
    all_cols = jnp.arange(col_owner.shape[0], dtype=jnp.int32)[None, :]
    local = jnp.sum((mine & (all_cols < blk_col[:, None])).astype(jnp.int32), axis=1)
    live = jnp.arange(slots, dtype=jnp.int32) < blk_count[0]
    col_tab, col_groups = group_table(local, blk_row, live, cols, n_rows)
    row_tab, row_groups = group_table(blk_row, local, live, n_rows, cols)
    n_groups = jnp.sum(col_groups)

    def as_meta(*values):
        return jnp.stack([jnp.asarray(v, jnp.int32) for v in values])

    xq = pl.pallas_call(
        quarter_kernel,
        out_shape=[jax.ShapeDtypeStruct((per, part, rows_tok), bf16)] * n_tok,
        in_specs=[SMEM, VMEM],
        out_specs=[VMEM] * n_tok,
        scratch_shapes=[pltpu.VMEM((per, block, rows_tok), bf16)],
        compiler_params=params,
    )(me_tok.astype(jnp.int32)[None], tokens)
    if fast:
        xq = [xq[0], tok(xq[1], TOK_X), tok(xq[2], TOK_Y), tok(xq[3], TOK_XY)]
        xq = jnp.concatenate(xq, axis=2)
        xq, _ = lax.optimization_barrier((xq, shards[-1]))
        xq_shards = gather_line(xq, middle)
    else:
        order = me_tok ^ jnp.arange(n_tok)
        xq = jnp.take(jnp.stack(xq), order, axis=0)
        xq = lax.all_to_all(xq, "tok", split_axis=0, concat_axis=0, tiled=True)
        xq = xq.transpose(1, 2, 0, 3).reshape(per, part, n_tok * rows_tok)
        xq_shards = [lax.all_gather(xq, "blk", axis=0, tiled=True)]

    cuts = (0, cols // 2)
    sizes = (cols // 2, cols - cols // 2)
    act, *hs = pl.pallas_call(
        functools.partial(forward_kernel, len(shards), cuts),
        out_shape=[jax.ShapeDtypeStruct(cotangent.shape, bf16)]
        + [jax.ShapeDtypeStruct((rows_tok, n * block), bf16) for n in sizes],
        in_specs=[SMEM, SMEM] + [ANY] * len(shards) + [VMEM, VMEM],
        out_specs=[VMEM] * (1 + len(sizes)),
        scratch_shapes=[
            pltpu.VMEM((n_blk + 1, rows_tok, width), bf16),
            pltpu.VMEM((cols, rows_tok, block), jnp.float32),
            pltpu.SemaphoreType.DMA((len(shards),)),
        ],
        compiler_params=params,
        name="forward",
    )(col_tab, as_meta(n_groups, 0, *panels), *shards, w_blocks, cotangent)

    if fast:
        (a, b) = hs
        ax, ay = tok(a, TOK_X), tok(a, TOK_Y)
        bx, by = tok(b, TOK_X), tok(b, TOK_Y)
        ad, bd = tok(ax, TOK_Y), tok(by, TOK_X)
        gathered = [[a, ax, ay, ad], [b, bx, by, bd]]
    else:
        gathered = [[lax.all_gather(h, "tok", axis=0)] for h in hs]

    if fast:
        outs = [4, 4]
        order = panels
    else:
        outs = [n_blk]
        order = list(range(n_blk))
    terms = pl.pallas_call(
        functools.partial(term_kernel, len(hs)),
        out_shape=[jax.ShapeDtypeStruct((n, rows_tok, width), bf16) for n in outs],
        in_specs=[SMEM, SMEM] + [VMEM] * (len(hs) + 1),
        out_specs=[VMEM] * len(outs),
        scratch_shapes=[
            pltpu.VMEM((rows_tok, (cols + 1) * block), bf16),
            pltpu.VMEM((n_rows, rows_tok, block), jnp.float32),
        ],
        compiler_params=params,
        name="term",
    )(row_tab, as_meta(jnp.sum(row_groups), 0, *order), *hs, w_blocks)

    def add(*xs):
        return sum(x.astype(jnp.float32) for x in xs).astype(bf16)

    if fast:
        keep, send = terms
        q = add(keep, blk(send, CORES))
        own, near, mid, last = (q[i] for i in range(4))
        a1 = blk(last, INWARD)
        b1 = blk(mid, INWARD)
        a2 = blk(add(last, a1), ODD)
        e3 = blk(add(near, a2), EVEN)
        o3 = blk(add(mid, b1), ODD)
        input_grad = add(own, e3, o3)
    else:
        input_grad = lax.psum_scatter(terms[0], "blk", scatter_dimension=0, tiled=True)[0]

    grad = None
    done = jnp.int32(0)
    for k, hk in enumerate(gathered):
        upto = done + jnp.sum(col_groups[cuts[k] : cuts[k] + sizes[k]])
        extra = [] if grad is None else [grad]
        if fast:
            x_panels = [p * per for p in panels]
        else:
            x_panels = [0]
        grad = pl.pallas_call(
            functools.partial(
                grad_kernel, None if grad is None else 0, len(xq_shards), cuts[k]
            ),
            out_shape=jax.ShapeDtypeStruct((slots, part, block), bf16),
            in_specs=[SMEM, SMEM] + [ANY] * len(xq_shards) + [VMEM] * (len(hk) + len(extra)),
            out_specs=VMEM,
            scratch_shapes=[
                pltpu.VMEM((n_rows, part, n_tok * rows_tok), bf16),
                pltpu.SemaphoreType.DMA((len(xq_shards),)),
            ],
            compiler_params=params,
            name="weight_grad",
        )(col_tab, as_meta(done, upto, *x_panels), *xq_shards, *hk, *extra)
        done = upto
    return act, input_grad, grad


def solution(mesh):
    return jax.shard_map(
        functools.partial(on_device, mesh.shape["tok"], mesh.shape["blk"]),
        mesh=mesh,
        in_specs=(
            P("tok", "blk"),
            P("blk", None, None),
            P("blk"),
            P("blk"),
            P("blk"),
            P(),
            P("tok", "blk"),
        ),
        out_specs=(P("tok", "blk"), P("tok", "blk"), P("blk", "tok", None)),
        check_vma=False,
    )
```

```python
import functools

import jax
import jax.numpy as jnp
from jax import lax
from jax.experimental import pallas as pl
from jax.experimental.pallas import tpu as pltpu
from jax.sharding import PartitionSpec as P


GROUP = 4
LIMIT = 16 * 1024 * 1024
VMEM = pl.BlockSpec(memory_space=pltpu.VMEM)
SMEM = pl.BlockSpec(memory_space=pltpu.SMEM)
ANY = pl.BlockSpec(memory_space=pl.ANY)
HBM = pl.BlockSpec(memory_space=pltpu.HBM)


def group_ranks(key, live, n_keys):
    ids = jnp.arange(key.shape[0], dtype=jnp.int32)
    keys = jnp.arange(n_keys, dtype=jnp.int32)
    same = (key[:, None] == key[None, :]) & (ids[None, :] < ids[:, None]) & live[None, :]
    rank = jnp.sum(same.astype(jnp.int32), axis=1)
    hit = (key[:, None] == keys[None, :]) & live[:, None]
    return rank, (jnp.sum(hit.astype(jnp.int32), axis=0) + GROUP - 1) // GROUP


def group_table(key, other, live, rank, groups, pad_other):
    slots, n_keys = key.shape[0], groups.shape[0]
    ids = jnp.arange(slots, dtype=jnp.int32)
    keys = jnp.arange(n_keys, dtype=jnp.int32)
    start = jnp.sum(jnp.where(keys[None, :] < key[:, None], groups[None, :], 0), axis=1)
    total = (slots + n_keys * (GROUP - 1) + GROUP - 1) // GROUP * GROUP
    place = jnp.where(live, start * GROUP + rank, total)
    pad = slots | (pad_other << 9)
    entry = ids | (other << 9) | (key << 16)
    at = jnp.arange(total, dtype=jnp.int32)
    return pad + jnp.sum(
        jnp.where(place[None, :] == at[:, None], (entry - pad)[None, :], 0), axis=1
    )


def each(lo, hi, body, unroll):
    n = hi - lo
    main = n // unroll

    def many(i, carry):
        for u in range(unroll):
            body(lo + i * unroll + u)
        return carry

    def one(i, carry):
        body(i)
        return carry

    lax.fori_loop(0, main, many, 0)
    lax.fori_loop(lo + main * unroll, hi, one, 0)


def unpack(tab, g):
    entries = [tab[g * GROUP + i] for i in range(GROUP)]
    return (
        [e & 511 for e in entries],
        [lax.shift_right_logical(e, 9) & 127 for e in entries],
        lax.shift_right_logical(entries[0], 16),
    )


def lanes(ref, at, i, block):
    return ref[at, :, pl.ds(pl.multiple_of(i * block, block), block)]


def forward_kernel(shards, cuts, tab, meta, *refs):
    x_in = refs[:shards]
    w_ref, cot_ref, act_ref = refs[shards : shards + 3]
    h_refs = refs[shards + 3 : -3]
    x_ref, acc, sem = refs[-3:]
    slots, block, _ = w_ref.shape
    per = x_ref.shape[2] // block
    cols = acc.shape[0]
    copies = []
    for i, ref in enumerate(x_in):
        n = ref.shape[0]
        copies.append(pltpu.make_async_copy(ref, x_ref.at[pl.ds(meta[4 + i], n)], sem.at[i]))
    for copy in copies:
        copy.start()
    acc[...] = jnp.zeros_like(acc)
    x_ref[x_ref.shape[0] - 1, :, 0:block] = jnp.zeros((x_ref.shape[1], block), x_ref.dtype)
    for copy in copies:
        copy.wait()

    def group(g):
        ids, rows, col = unpack(tab, g)
        x = jnp.concatenate([lanes(x_ref, r // per, r % per, block) for r in rows], axis=1)
        w = jnp.concatenate([w_ref[jnp.minimum(s, slots - 1)] for s in ids], axis=0)
        acc[col] += jnp.dot(x, w, preferred_element_type=jnp.float32)

    each(0, meta[0], group, 4)
    for c in range(cols):
        at = slice(c * block, (c + 1) * block)
        hidden = acc[c]
        gate = jax.nn.sigmoid(hidden)
        act_ref[:, at] = (hidden * gate).astype(act_ref.dtype)
        slope = gate * (1.0 + hidden * (1.0 - gate))
        grad = (cot_ref[:, at].astype(jnp.float32) * slope).astype(act_ref.dtype)
        k = max(i for i in range(len(cuts)) if cuts[i] <= c)
        h_refs[k][:, (c - cuts[k]) * block : (c - cuts[k] + 1) * block] = grad


def term_kernel(chunks, ordered, tab, meta, *refs):
    h_in = refs[:chunks]
    w_ref = refs[chunks]
    outs = refs[chunks + 1 : -2]
    h_ref, acc = refs[-2:]
    slots, block, _ = w_ref.shape
    acc[...] = jnp.zeros_like(acc)
    at = 0
    for ref in h_in:
        h_ref[:, at : at + ref.shape[1]] = ref[...]
        at += ref.shape[1]
    h_ref[:, at : at + block] = jnp.zeros((h_ref.shape[0], block), h_ref.dtype)

    def group(g):
        ids, cols, row = unpack(tab, g)
        h = jnp.concatenate(
            [h_ref[:, pl.ds(pl.multiple_of(c * block, block), block)] for c in cols], axis=1
        )
        w = jnp.concatenate([w_ref[jnp.minimum(s, slots - 1)] for s in ids], axis=1)
        acc[row] += lax.dot_general(
            h, w, (((1,), (1,)), ((), ())), preferred_element_type=jnp.float32
        )

    each(0, meta[1], group, 4)
    role = 0
    for ref in outs:
        for i in range(ref.shape[0]):
            panel = meta[4 + role] if ordered else role
            per = ref.shape[2] // block
            for j in range(per):
                ref[i, :, j * block : (j + 1) * block] = acc[panel * per + j].astype(ref.dtype)
            role += 1


def grad_kernel(second, shards, base_col, per, tab, meta, *refs):
    x_in = refs[:shards]
    h_in = refs[shards : -3]
    out_ref, x_ref, sem = refs[-3:]
    if second:
        h_in, old_ref = h_in[:-1], h_in[-1]
    block = out_ref.shape[2]
    part = out_ref.shape[1]
    copies = []
    for i, ref in enumerate(x_in):
        n = ref.shape[0]
        copies.append(pltpu.make_async_copy(ref, x_ref.at[pl.ds(meta[4 + i] * per, n)], sem.at[i]))
    for copy in copies:
        copy.start()
    if second:
        out_ref[...] = old_ref[...]
    else:
        out_ref[...] = jnp.zeros_like(out_ref)
    for copy in copies:
        copy.wait()

    def group(g):
        ids, rows, col = unpack(tab, g)
        first = ids[0]
        live = [s < out_ref.shape[0] for s in ids]
        ids = [jnp.where(l, s, first) for l, s in zip(live, ids)]
        rows = [jnp.where(l, r, rows[0]) for l, r in zip(live, rows)]
        x = jnp.concatenate([x_ref[r] for r in rows], axis=0)
        h = []
        for ref in h_in:
            at = pl.ds(pl.multiple_of((col - base_col) * block, block), block)
            if len(ref.shape) == 2:
                h.append(ref[:, at])
            else:
                h += [ref[i, :, at] for i in range(ref.shape[0])]
        h = jnp.concatenate(h, axis=0)
        out = jnp.dot(x, h, preferred_element_type=jnp.float32).astype(out_ref.dtype)
        for i, s in enumerate(ids):
            out_ref[s] = out[i * part : (i + 1) * part]

    lo, hi = (meta[2], meta[0]) if second else (0, meta[2])
    each(lo, hi, group, 4)


def quarter_kernel(me, tok_ref, *refs):
    outs, scratch = refs[:-1], refs[-1]
    block = scratch.shape[1]
    part = outs[0].shape[1]
    for r in range(scratch.shape[0]):
        scratch[r] = tok_ref[:, r * block : (r + 1) * block].T
    for j, ref in enumerate(outs):
        at = pl.multiple_of((me[0] ^ j) * part, part)
        ref[...] = scratch[:, pl.ds(at, part), :]


def along_z(pairs):
    return [(a * 2 + c, b * 2 + c) for a, b in pairs for c in range(2)]


EVEN = along_z([(0, 1), (1, 0), (2, 3), (3, 2)])
ODD = along_z([(1, 2), (2, 1)])
OUTWARD = along_z([(1, 0), (2, 3)])
INWARD = along_z([(0, 1), (3, 2)])
CORES = [(b, b ^ 1) for b in range(8)]
TOK_X = [(t, t ^ 1) for t in range(4)]
TOK_Y = [(t, t ^ 2) for t in range(4)]
TOK_XY = [(t, t ^ 3) for t in range(4)]


def blk(x, pairs):
    return lax.ppermute(x, "blk", pairs)


def tok(x, pairs):
    return lax.ppermute(x, "tok", pairs)


def gather_line(x, middle):
    e1, o1 = blk(x, EVEN), blk(x, ODD)
    p0 = blk(x, CORES)
    o2, e2 = blk(e1, ODD), blk(o1, OUTWARD)
    p1 = blk(e1, CORES)
    e3 = blk(o2, OUTWARD)
    n2 = jnp.where(middle, o1, e2)
    p2 = blk(n2, CORES)
    n3 = jnp.where(middle, o2, e3)
    p3 = blk(n3, CORES)
    return [x, e1, n2, n3, p0, p1, p2, p3]


def on_device(n_tok, n_blk, tokens, w_blocks, blk_row, blk_col, blk_count, col_owner, cotangent):
    fast = (n_tok, n_blk) == (4, 8)
    rows_tok, width = tokens.shape
    slots, block, _ = w_blocks.shape
    cols = cotangent.shape[1] // block
    per = width // block
    n_rows = per * n_blk
    part = block // n_tok
    me_blk = lax.axis_index("blk")
    me_tok = lax.axis_index("tok")
    z, core = me_blk // 2, me_blk % 2
    middle = (z == 1) | (z == 2)
    bf16 = tokens.dtype
    params = pltpu.CompilerParams(vmem_limit_bytes=LIMIT)

    if fast:
        far = [z, z ^ 1, jnp.where(z < 2, 2, 1), jnp.where(z < 2, 3, 0)]
        panels = [f * 2 + core for f in far] + [f * 2 + 1 - core for f in far]
        shards = gather_line(tokens, middle)
        shards = [s[None] for s in shards]
    else:
        panels = [jnp.int32(0)]
        shards = [lax.all_gather(tokens, "blk", axis=0)]

    mine = (col_owner == me_blk)[None, :]
    all_cols = jnp.arange(col_owner.shape[0], dtype=jnp.int32)[None, :]
    local = jnp.sum((mine & (all_cols < blk_col[:, None])).astype(jnp.int32), axis=1)
    live = jnp.arange(slots, dtype=jnp.int32) < blk_count[0]
    col_rank, col_groups = group_ranks(local, live, cols)
    row_rank, row_groups = group_ranks(blk_row, live, n_rows)
    cuts = (0, cols // 2)
    sizes = (cols // 2, cols - cols // 2)
    col_tab = group_table(local, blk_row, live, col_rank, col_groups, n_rows)
    row_tab = group_table(blk_row, local, live, row_rank, row_groups, cols)
    values = [jnp.sum(col_groups), jnp.sum(row_groups), jnp.sum(col_groups[: cuts[1]]), me_tok]
    meta = jnp.stack([jnp.asarray(v, jnp.int32) for v in values + panels])

    xq = pl.pallas_call(
        quarter_kernel,
        out_shape=[jax.ShapeDtypeStruct((per, part, rows_tok), bf16)] * n_tok,
        in_specs=[SMEM, VMEM],
        out_specs=[VMEM] * n_tok,
        scratch_shapes=[pltpu.VMEM((per, block, rows_tok), bf16)],
        compiler_params=params,
        name="quarter",
    )(me_tok.astype(jnp.int32)[None], tokens)
    if fast:
        xq = [xq[0], tok(xq[1], TOK_X), tok(xq[2], TOK_Y), tok(xq[3], TOK_XY)]
        xq = jnp.concatenate(xq, axis=2)
        xq_shards = gather_line(xq, middle)
    else:
        order = me_tok ^ jnp.arange(n_tok)
        xq = jnp.take(jnp.stack(xq), order, axis=0)
        xq = lax.all_to_all(xq, "tok", split_axis=0, concat_axis=0, tiled=True)
        xq = xq.transpose(1, 2, 0, 3).reshape(per, part, n_tok * rows_tok)
        xq_shards = [lax.all_gather(xq, "blk", axis=0, tiled=True)]

    act, *hs = pl.pallas_call(
        functools.partial(forward_kernel, len(shards), cuts),
        out_shape=[jax.ShapeDtypeStruct(cotangent.shape, bf16)]
        + [jax.ShapeDtypeStruct((rows_tok, n * block), bf16) for n in sizes],
        in_specs=[SMEM, SMEM] + [ANY] * len(shards) + [VMEM, VMEM],
        out_specs=[VMEM] * (1 + len(sizes)),
        scratch_shapes=[
            pltpu.VMEM((n_blk + 1, rows_tok, width), bf16),
            pltpu.VMEM((cols, rows_tok, block), jnp.float32),
            pltpu.SemaphoreType.DMA((len(shards),)),
        ],
        compiler_params=params,
        name="forward",
    )(col_tab, meta, *shards, w_blocks, cotangent)

    if fast:
        (a, b) = hs
        ax, ay = tok(a, TOK_X), tok(a, TOK_Y)
        bx, by = tok(b, TOK_X), tok(b, TOK_Y)
        ad, bd = tok(ax, TOK_Y), tok(by, TOK_X)
        gathered = [[a, ax, ay, ad], [b, bx, by, bd]]
    else:
        gathered = [[lax.all_gather(h, "tok", axis=0)] for h in hs]

    if fast:
        outs = [4, 4]
    else:
        outs = [n_blk]
    terms = pl.pallas_call(
        functools.partial(term_kernel, len(hs), fast),
        out_shape=[jax.ShapeDtypeStruct((n, rows_tok, width), bf16) for n in outs],
        in_specs=[SMEM, SMEM] + [VMEM] * (len(hs) + 1),
        out_specs=[VMEM] * len(outs),
        scratch_shapes=[
            pltpu.VMEM((rows_tok, (cols + 1) * block), bf16),
            pltpu.VMEM((n_rows, rows_tok, block), jnp.float32),
        ],
        compiler_params=params,
        name="term",
    )(row_tab, meta, *hs, w_blocks)

    def add(*xs):
        return sum(x.astype(jnp.float32) for x in xs).astype(bf16)

    if fast:
        keep, send = terms
        q = add(keep, blk(send, CORES))
        own, near, mid, last = (q[i] for i in range(4))
        a1 = blk(last, INWARD)
        b1 = blk(mid, INWARD)
        a2 = blk(add(last, a1), ODD)
        e3 = blk(add(near, a2), EVEN)
        o3 = blk(add(mid, b1), ODD)
        input_grad = add(own, e3, o3)
    else:
        input_grad = lax.psum_scatter(terms[0], "blk", scatter_dimension=0, tiled=True)[0]

    grad = None
    for k, hk in enumerate(gathered):
        extra = [] if grad is None else [grad]
        grad = pl.pallas_call(
            functools.partial(grad_kernel, k > 0, len(xq_shards), cuts[k], per),
            out_shape=jax.ShapeDtypeStruct((slots, part, block), bf16),
            in_specs=[SMEM, SMEM] + [ANY] * len(xq_shards) + [VMEM] * (len(hk) + len(extra)),
            out_specs=VMEM,
            scratch_shapes=[
                pltpu.VMEM((n_rows, part, n_tok * rows_tok), bf16),
                pltpu.SemaphoreType.DMA((len(xq_shards),)),
            ],
            compiler_params=params,
            name="weight_grad",
        )(col_tab, meta, *xq_shards, *hk, *extra)
    return act, input_grad, grad


def solution(mesh):
    n_tok, n_blk = mesh.shape["tok"], mesh.shape["blk"]

    def body(*args):
        return on_device(n_tok, n_blk, *args)

    return jax.shard_map(
        body,
        mesh=mesh,
        in_specs=(
            P("tok", "blk"),
            P("blk", None, None),
            P("blk"),
            P("blk"),
            P("blk"),
            P(),
            P("tok", "blk"),
        ),
        out_specs=(P("tok", "blk"), P("tok", "blk"), P("blk", "tok", None)),
        check_vma=False,
    )
```

```python
import functools

import jax
import jax.numpy as jnp
from jax import lax
from jax.experimental import pallas as pl
from jax.experimental.pallas import tpu as pltpu
from jax.sharding import PartitionSpec as P


GROUP = 4
LIMIT = 16 * 1024 * 1024
VMEM = pl.BlockSpec(memory_space=pltpu.VMEM)
SMEM = pl.BlockSpec(memory_space=pltpu.SMEM)
ANY = pl.BlockSpec(memory_space=pl.ANY)
HBM = pl.BlockSpec(memory_space=pltpu.HBM)


def group_ranks(key, live, n_keys):
    ids = jnp.arange(key.shape[0], dtype=jnp.int32)
    keys = jnp.arange(n_keys, dtype=jnp.int32)
    same = (key[:, None] == key[None, :]) & (ids[None, :] < ids[:, None]) & live[None, :]
    rank = jnp.sum(same.astype(jnp.int32), axis=1)
    hit = (key[:, None] == keys[None, :]) & live[:, None]
    return rank, (jnp.sum(hit.astype(jnp.int32), axis=0) + GROUP - 1) // GROUP


def group_table(key, other, live, rank, groups, pad_other):
    slots, n_keys = key.shape[0], groups.shape[0]
    ids = jnp.arange(slots, dtype=jnp.int32)
    keys = jnp.arange(n_keys, dtype=jnp.int32)
    start = jnp.sum(jnp.where(keys[None, :] < key[:, None], groups[None, :], 0), axis=1)
    total = (slots + n_keys * (GROUP - 1) + GROUP - 1) // GROUP * GROUP
    place = jnp.where(live, start * GROUP + rank, total)
    pad = slots | (pad_other << 9)
    entry = ids | (other << 9) | (key << 16)
    at = jnp.arange(total, dtype=jnp.int32)
    return pad + jnp.sum(
        jnp.where(place[None, :] == at[:, None], (entry - pad)[None, :], 0), axis=1
    )


def each(lo, hi, body, unroll):
    n = hi - lo
    main = n // unroll

    def many(i, carry):
        for u in range(unroll):
            body(lo + i * unroll + u)
        return carry

    def one(i, carry):
        body(i)
        return carry

    lax.fori_loop(0, main, many, 0)
    lax.fori_loop(lo + main * unroll, hi, one, 0)


def unpack(tab, g):
    entries = [tab[g * GROUP + i] for i in range(GROUP)]
    return (
        [e & 511 for e in entries],
        [lax.shift_right_logical(e, 9) & 127 for e in entries],
        lax.shift_right_logical(entries[0], 16),
    )


def lanes(ref, i, block):
    return ref[:, pl.ds(pl.multiple_of(i * block, block), block)]


def panels_of(me, n):
    if n == 1:
        return [0]
    z, core = lax.shift_right_logical(me, 1), me & 1
    far = [z, z ^ 1, jnp.where(z < 2, 2, 1), jnp.where(z < 2, 3, 0)]
    return [f * 2 + core for f in far] + [f * 2 + 1 - core for f in far]


def total(groups, lo, hi):
    n = jnp.int32(0)
    for i in range(lo, hi):
        n += groups[i]
    return n


def copy_shards(shards, dst, me, per, sem):
    copies = []
    for i, (ref, panel) in enumerate(zip(shards, panels_of(me, len(shards)))):
        at = dst.at[pl.ds(panel * per, ref.shape[0])]
        copies.append(pltpu.make_async_copy(ref, at, sem.at[i]))
    for copy in copies:
        copy.start()
    return copies


def forward_kernel(shards, start, stop, tab, groups, me, *refs):
    if shards:
        x_in, refs = refs[:shards], refs[shards:]
        w_ref, cot_ref, act_out, h_ref, x_ref, acc, act_ref, sems = refs
        copies = copy_shards(x_in, x_ref, me[0], 1, sems)
    else:
        x_ref, w_ref, cot_ref, _, act_out, h_ref, acc, act_ref, sems = refs
        copies = []
    slots, block, _ = w_ref.shape
    per = x_ref.shape[2] // block
    acc[...] = jnp.zeros_like(acc)
    if shards:
        x_ref[x_ref.shape[0] - 1, :, 0:block] = jnp.zeros((x_ref.shape[1], block), x_ref.dtype)
    lo = total(groups, 0, start)
    hi = lo + total(groups, start, stop)
    for copy in copies:
        copy.wait()

    def group(g):
        ids, rows, col = unpack(tab, g)
        x = jnp.concatenate([lanes(x_ref.at[r // per], r % per, block) for r in rows], axis=1)
        w = jnp.concatenate([w_ref[jnp.minimum(s, slots - 1)] for s in ids], axis=0)
        acc[col - start] += jnp.dot(x, w, preferred_element_type=jnp.float32)

    each(lo, hi, group, 4)
    for c in range(stop - start):
        at = slice(c * block, (c + 1) * block)
        hidden = acc[c]
        gate = jax.nn.sigmoid(hidden)
        act_ref[:, at] = (hidden * gate).astype(act_ref.dtype)
        slope = gate * (1.0 + hidden * (1.0 - gate))
        cot = cot_ref[:, (start + c) * block : (start + c + 1) * block]
        h_ref[:, at] = (cot.astype(jnp.float32) * slope).astype(h_ref.dtype)
    copy = pltpu.make_async_copy(
        act_ref, act_out.at[:, start * block : stop * block], sems.at[sems.shape[0] - 1]
    )
    copy.start()
    copy.wait()


def term_kernel(chunks, fast, tab, groups, me, *refs):
    h_in = refs[:chunks]
    w_ref = refs[chunks]
    outs = refs[chunks + 1 : -2]
    h_ref, acc = refs[-2:]
    slots, block, _ = w_ref.shape
    acc[...] = jnp.zeros_like(acc)
    at = 0
    for ref in h_in:
        h_ref[:, at : at + ref.shape[1]] = ref[...]
        at += ref.shape[1]
    h_ref[:, at : at + block] = jnp.zeros((h_ref.shape[0], block), h_ref.dtype)

    def group(g):
        ids, cols, row = unpack(tab, g)
        h = jnp.concatenate([lanes(h_ref, c, block) for c in cols], axis=1)
        w = jnp.concatenate([w_ref[jnp.minimum(s, slots - 1)] for s in ids], axis=1)
        acc[row] += lax.dot_general(
            h, w, (((1,), (1,)), ((), ())), preferred_element_type=jnp.float32
        )

    each(0, total(groups, 0, groups.shape[0]), group, 4)
    panels = panels_of(me[0], 8) if fast else list(range(outs[0].shape[0]))
    for ref in outs:
        for i in range(ref.shape[0]):
            panel = panels.pop(0)
            per = ref.shape[2] // block
            for j in range(per):
                ref[i, :, j * block : (j + 1) * block] = acc[panel * per + j].astype(ref.dtype)


def grad_kernel(first, shards, heads, cuts, tokens, per, tab, groups, me, count, *refs):
    if first:
        x_in, refs = refs[:shards], refs[shards:]
    else:
        x_ref, sum_ref, refs = refs[0], refs[1], refs[2:]
    n = sum(heads)
    h_in, refs = refs[:n], refs[n:]
    out_ref = refs[0]
    copies = []
    if first:
        x_ref, sems = refs[1:]
        copies = copy_shards(x_in, x_ref, me[0], per, sems)
    slots, part, block = out_ref.shape

    def clear(s, carry):
        out_ref[s] = jnp.zeros((part, block), out_ref.dtype)
        return carry

    lax.fori_loop(jnp.minimum(count[0], slots), slots, clear, 0)
    for copy in copies:
        copy.wait()
    lo = jnp.int32(0)
    for k, head in enumerate(heads):
        mine, h_in = h_in[:head], h_in[head:]
        hi = lo + total(groups, cuts[k], cuts[k + 1])

        def group(g):
            ids, rows, col = unpack(tab, g)
            live = [s < slots for s in ids]
            ids = [jnp.where(l, s, ids[0]) for l, s in zip(live, ids)]
            rows = [jnp.where(l, r, rows[0]) for l, r in zip(live, rows)]
            x = jnp.concatenate([x_ref[r, :, tokens] for r in rows], axis=0)
            h = []
            for ref in mine:
                views = [ref] if len(ref.shape) == 2 else [ref.at[i] for i in range(ref.shape[0])]
                h += [lanes(v, col - cuts[k], block) for v in views]
            h = jnp.concatenate(h, axis=0)
            out = jnp.dot(x, h, preferred_element_type=jnp.float32)
            if not first:
                out += jnp.concatenate([sum_ref[s] for s in ids], axis=0)
            out = out.astype(out_ref.dtype)
            for i, s in enumerate(ids):
                out_ref[s] = out[i * part : (i + 1) * part]

        each(lo, hi, group, 4)
        lo = hi


def quarter_kernel(me, tok_ref, *refs):
    outs, scratch = refs[:-1], refs[-1]
    block = scratch.shape[1]
    part = outs[0].shape[1]
    for r in range(scratch.shape[0]):
        scratch[r] = tok_ref[:, r * block : (r + 1) * block].T
    for j, ref in enumerate(outs):
        at = pl.multiple_of((me[0] ^ j) * part, part)
        ref[...] = scratch[:, pl.ds(at, part), :]


def warm_kernel(w_ref, out_ref, sem):
    copy = pltpu.make_async_copy(w_ref.at[0, 0:8], out_ref, sem)
    copy.start()
    copy.wait()


def join_kernel(*refs):
    refs[-1][...] = jnp.concatenate([ref[...] for ref in refs[:-1]], axis=2)


def along_z(pairs):
    return [(a * 2 + c, b * 2 + c) for a, b in pairs for c in range(2)]


EVEN = along_z([(0, 1), (1, 0), (2, 3), (3, 2)])
ODD = along_z([(1, 2), (2, 1)])
OUTWARD = along_z([(1, 0), (2, 3)])
INWARD = along_z([(0, 1), (3, 2)])
CORES = [(b, b ^ 1) for b in range(8)]
TOK_X = [(t, t ^ 1) for t in range(4)]
TOK_Y = [(t, t ^ 2) for t in range(4)]
TOK_XY = [(t, t ^ 3) for t in range(4)]


def blk(x, pairs):
    return lax.ppermute(x, "blk", pairs)


def tok(x, pairs):
    return lax.ppermute(x, "tok", pairs)


def gather_line(x, middle):
    e1, o1 = blk(x, EVEN), blk(x, ODD)
    p0 = blk(x, CORES)
    o2, e2 = blk(e1, ODD), blk(o1, OUTWARD)
    p1 = blk(e1, CORES)
    e3 = blk(o2, OUTWARD)
    n2 = jnp.where(middle, o1, e2)
    p2 = blk(n2, CORES)
    n3 = jnp.where(middle, o2, e3)
    p3 = blk(n3, CORES)
    return [x, e1, n2, n3, p0, p1, p2, p3]


def call(body, out_shape, in_specs, out_specs, scratch, side=False, **kwargs):
    return pl.pallas_call(
        body,
        out_shape=out_shape,
        in_specs=in_specs,
        out_specs=out_specs,
        scratch_shapes=scratch,
        compiler_params=pltpu.CompilerParams(vmem_limit_bytes=LIMIT, has_side_effects=side),
        **kwargs,
    )


def on_device(n_tok, n_blk, tokens, w_blocks, blk_row, blk_col, blk_count, col_owner, cotangent):
    fast = (n_tok, n_blk) == (4, 8)
    rows_tok, width = tokens.shape
    slots, block, _ = w_blocks.shape
    cols = cotangent.shape[1] // block
    per = width // block
    n_rows = per * n_blk
    part = block // n_tok
    me_blk = lax.axis_index("blk").astype(jnp.int32)
    me_tok = lax.axis_index("tok").astype(jnp.int32)
    z = me_blk // 2
    middle = (z == 1) | (z == 2)
    me = me_blk[None]
    bf16 = tokens.dtype

    def shape(*dims, dtype=bf16):
        return jax.ShapeDtypeStruct(dims, dtype)

    if fast:
        shards = [s[None] for s in gather_line(tokens, middle)]
    else:
        shards = [lax.all_gather(tokens, "blk", axis=0)]

    mine = (col_owner == me_blk)[None, :]
    all_cols = jnp.arange(col_owner.shape[0], dtype=jnp.int32)[None, :]
    local = jnp.sum((mine & (all_cols < blk_col[:, None])).astype(jnp.int32), axis=1)
    live = jnp.arange(slots, dtype=jnp.int32) < blk_count[0]
    col_rank, col_groups = group_ranks(local, live, cols)
    row_rank, row_groups = group_ranks(blk_row, live, n_rows)
    col_tab = group_table(local, blk_row, live, col_rank, col_groups, n_rows)
    row_tab = group_table(blk_row, local, live, row_rank, row_groups, cols)

    xq = call(
        quarter_kernel,
        [shape(per, part, rows_tok)] * n_tok,
        [SMEM, VMEM],
        [VMEM] * n_tok,
        [pltpu.VMEM((per, block, rows_tok), bf16)],
    )(me_tok[None], tokens)
    if fast:
        moved = [tok(xq[1], TOK_X), tok(xq[2], TOK_Y), tok(xq[3], TOK_XY)]
        xq = call(
            join_kernel, shape(per, part, n_tok * rows_tok), [VMEM] * n_tok, VMEM, []
        )(xq[0], *moved)
        xq_shards = gather_line(xq, middle)
    else:
        order = me_tok ^ jnp.arange(n_tok)
        xq = jnp.take(jnp.stack(xq), order, axis=0)
        xq = lax.all_to_all(xq, "tok", split_axis=0, concat_axis=0, tiled=True)
        xq = xq.transpose(1, 2, 0, 3).reshape(per, part, n_tok * rows_tok)
        xq_shards = [lax.all_gather(xq, "blk", axis=0, tiled=True)]

    call(warm_kernel, shape(8, block), [HBM], VMEM, [pltpu.SemaphoreType.DMA], side=True)(w_blocks)

    cuts = (0, cols // 2, cols)
    hs = []
    x_all = act = None
    for k, (start, stop) in enumerate(zip(cuts[:-1], cuts[1:])):
        n = stop - start
        outs = [shape(*cotangent.shape), shape(rows_tok, n * block)]
        scratch = [
            pltpu.VMEM((n, rows_tok, block), jnp.float32),
            pltpu.VMEM((rows_tok, n * block), bf16),
        ]
        if k == 0:
            act, h, x_all = call(
                functools.partial(forward_kernel, len(shards), start, stop),
                outs + [shape(n_blk + 1, rows_tok, width)],
                [SMEM] * 3 + [ANY] * len(shards) + [VMEM, VMEM],
                [HBM, VMEM, VMEM],
                scratch + [pltpu.SemaphoreType.DMA((len(shards) + 1,))],
            )(col_tab, col_groups, me, *shards, w_blocks, cotangent)
        else:
            act, h = call(
                functools.partial(forward_kernel, 0, start, stop),
                outs,
                [SMEM] * 3 + [VMEM, VMEM, VMEM, HBM],
                [HBM, VMEM],
                scratch + [pltpu.SemaphoreType.DMA((1,))],
                input_output_aliases={6: 0},
            )(col_tab, col_groups, me, x_all, w_blocks, cotangent, act)
        hs.append(h)

    if fast:
        (a, b) = hs
        ax, ay = tok(a, TOK_X), tok(a, TOK_Y)
        bx, by = tok(b, TOK_X), tok(b, TOK_Y)
        ad, bd = tok(ax, TOK_Y), tok(by, TOK_X)
        near, far = [[a, ax, ay], [b, bx, by]], [[ad], [bd]]
    else:
        near, far = [[lax.all_gather(h, "tok", axis=0)] for h in hs], None

    outs = [4, 4] if fast else [n_blk]
    terms = call(
        functools.partial(term_kernel, len(hs), fast),
        [shape(n, rows_tok, width) for n in outs],
        [SMEM] * 3 + [VMEM] * (len(hs) + 1),
        [VMEM] * len(outs),
        [
            pltpu.VMEM((rows_tok, (cols + 1) * block), bf16),
            pltpu.VMEM((n_rows, rows_tok, block), jnp.float32),
        ],
    )(row_tab, row_groups, me, *hs, w_blocks)

    def add(*xs):
        return sum(x.astype(jnp.float32) for x in xs).astype(bf16)

    if fast:
        keep, send = terms
        q = add(keep, blk(send, CORES))
        own, close, mid, last = (q[i] for i in range(4))
        a1 = blk(last, INWARD)
        b1 = blk(mid, INWARD)
        a2 = blk(add(last, a1), ODD)
        e3 = blk(add(close, a2), EVEN)
        o3 = blk(add(mid, b1), ODD)
        input_grad = add(own, e3, o3)
    else:
        input_grad = lax.psum_scatter(terms[0], "blk", scatter_dimension=0, tiled=True)[0]

    n_tokens = n_tok * rows_tok
    split = n_tokens - rows_tok if fast else n_tokens
    tables = (col_tab, col_groups, me, blk_count)
    x_shape = (n_rows, part, n_tokens)
    heads = [len(h) for h in near]
    grad, xq_all = call(
        functools.partial(grad_kernel, True, len(xq_shards), heads, cuts, slice(0, split), per),
        [shape(slots, part, block, dtype=jnp.float32 if fast else bf16), shape(*x_shape)],
        [SMEM] * 4 + [ANY] * len(xq_shards) + [VMEM] * sum(heads),
        [VMEM, VMEM],
        [pltpu.SemaphoreType.DMA((len(xq_shards),))],
    )(*tables, *xq_shards, *sum(near, []))
    if fast:
        heads = [len(h) for h in far]
        grad = call(
            functools.partial(grad_kernel, False, 0, heads, cuts, slice(split, n_tokens), per),
            shape(slots, part, block),
            [SMEM] * 4 + [VMEM] * (2 + sum(heads)),
            VMEM,
            [],
        )(*tables, xq_all, grad, *sum(far, []))
    return act, input_grad, grad


def solution(mesh):
    n_tok, n_blk = mesh.shape["tok"], mesh.shape["blk"]

    def body(*args):
        return on_device(n_tok, n_blk, *args)

    return jax.shard_map(
        body,
        mesh=mesh,
        in_specs=(
            P("tok", "blk"),
            P("blk", None, None),
            P("blk"),
            P("blk"),
            P("blk"),
            P(),
            P("tok", "blk"),
        ),
        out_specs=(P("tok", "blk"), P("tok", "blk"), P("blk", "tok", None)),
        check_vma=False,
    )
```

```python
import functools

import jax
import jax.numpy as jnp
from jax import lax
from jax.experimental import pallas as pl
from jax.experimental.pallas import tpu as pltpu
from jax.sharding import PartitionSpec as P


GROUP = 4
LIMIT = 16 * 1024 * 1024
VMEM = pl.BlockSpec(memory_space=pltpu.VMEM)
SMEM = pl.BlockSpec(memory_space=pltpu.SMEM)
ANY = pl.BlockSpec(memory_space=pl.ANY)
HBM = pl.BlockSpec(memory_space=pltpu.HBM)


def group_ranks(key, live, n_keys):
    ids = jnp.arange(key.shape[0], dtype=jnp.int32)
    keys = jnp.arange(n_keys, dtype=jnp.int32)
    same = (key[:, None] == key[None, :]) & (ids[None, :] < ids[:, None]) & live[None, :]
    rank = jnp.sum(same.astype(jnp.int32), axis=1)
    hit = (key[:, None] == keys[None, :]) & live[:, None]
    return rank, (jnp.sum(hit.astype(jnp.int32), axis=0) + GROUP - 1) // GROUP


def group_table(key, other, live, rank, groups, pad_other):
    slots, n_keys = key.shape[0], groups.shape[0]
    ids = jnp.arange(slots, dtype=jnp.int32)
    keys = jnp.arange(n_keys, dtype=jnp.int32)
    start = jnp.sum(jnp.where(keys[None, :] < key[:, None], groups[None, :], 0), axis=1)
    total = (slots + n_keys * (GROUP - 1) + GROUP - 1) // GROUP * GROUP
    place = jnp.where(live, start * GROUP + rank, total)
    pad = slots | (pad_other << 9)
    entry = ids | (other << 9) | (key << 16)
    at = jnp.arange(total, dtype=jnp.int32)
    return pad + jnp.sum(
        jnp.where(place[None, :] == at[:, None], (entry - pad)[None, :], 0), axis=1
    )


def each(lo, hi, body, unroll):
    n = hi - lo
    main = n // unroll

    def many(i, carry):
        for u in range(unroll):
            body(lo + i * unroll + u)
        return carry

    def one(i, carry):
        body(i)
        return carry

    lax.fori_loop(0, main, many, 0)
    lax.fori_loop(lo + main * unroll, hi, one, 0)


def unpack(tab, g):
    entries = [tab[g * GROUP + i] for i in range(GROUP)]
    return (
        [e & 511 for e in entries],
        [lax.shift_right_logical(e, 9) & 127 for e in entries],
        lax.shift_right_logical(entries[0], 16),
    )


def lanes(ref, i, block):
    return ref[:, pl.ds(pl.multiple_of(i * block, block), block)]


def panels_of(me, n):
    if n == 1:
        return [0]
    z, core = lax.shift_right_logical(me, 1), me & 1
    far = [z, z ^ 1, jnp.where(z < 2, 2, 1), jnp.where(z < 2, 3, 0)]
    return [f * 2 + core for f in far] + [f * 2 + 1 - core for f in far]


def total(groups, lo, hi):
    n = jnp.int32(0)
    for i in range(lo, hi):
        n += groups[i]
    return n


def copy_shards(shards, dst, me, per, sems):
    whole = len(shards) == 1
    panels = panels_of(me, 1 if whole else 8)
    copies = []
    for ref in shards:
        n = ref.shape[0] if whole else per
        for i in range(ref.shape[0] // n):
            at = dst.at[pl.ds(panels.pop(0) * per, n)]
            sem = sems.at[len(copies)]
            copies.append(pltpu.make_async_copy(ref.at[pl.ds(i * n, n)], at, sem))
    for copy in copies:
        copy.start()
    return copies


def forward_kernel(shards, start, stop, tab, groups, me, *refs):
    if shards:
        x_in, refs = refs[:shards], refs[shards:]
        w_ref, cot_ref, act_ref, h_ref, x_ref, acc, sems = refs
        copies = copy_shards(x_in, x_ref, me[0], 1, sems)
    else:
        x_ref, w_ref, cot_ref, before, act_out, h_ref, acc, act_ref, sems = refs
        copies = []
    slots, block, _ = w_ref.shape
    per = x_ref.shape[2] // block
    if not shards:
        left = pltpu.make_async_copy(before, act_out.at[:, : start * block], sems.at[0])
        left.start()
    acc[...] = jnp.zeros_like(acc)
    if shards:
        x_ref[x_ref.shape[0] - 1, :, 0:block] = jnp.zeros((x_ref.shape[1], block), x_ref.dtype)
    lo = total(groups, 0, start)
    hi = lo + total(groups, start, stop)
    for copy in copies:
        copy.wait()

    def group(g):
        ids, rows, col = unpack(tab, g)
        x = jnp.concatenate([lanes(x_ref.at[r // per], r % per, block) for r in rows], axis=1)
        w = jnp.concatenate([w_ref[jnp.minimum(s, slots - 1)] for s in ids], axis=0)
        acc[col - start] += jnp.dot(x, w, preferred_element_type=jnp.float32)

    each(lo, hi, group, 4)
    for c in range(stop - start):
        at = slice(c * block, (c + 1) * block)
        hidden = acc[c]
        gate = jax.nn.sigmoid(hidden)
        act_ref[:, at] = (hidden * gate).astype(act_ref.dtype)
        slope = gate * (1.0 + hidden * (1.0 - gate))
        cot = cot_ref[:, (start + c) * block : (start + c + 1) * block]
        h_ref[:, at] = (cot.astype(jnp.float32) * slope).astype(h_ref.dtype)
    if not shards:
        right = pltpu.make_async_copy(
            act_ref, act_out.at[:, start * block : stop * block], sems.at[1]
        )
        right.start()
        left.wait()
        right.wait()


def term_kernel(chunks, fast, tab, groups, me, *refs):
    h_in = refs[:chunks]
    w_ref = refs[chunks]
    outs = refs[chunks + 1 : -2]
    h_ref, acc = refs[-2:]
    slots, block, _ = w_ref.shape
    per = outs[0].shape[2] // block
    acc[...] = jnp.zeros_like(acc)
    at = 0
    for ref in h_in:
        h_ref[:, at : at + ref.shape[1]] = ref[...]
        at += ref.shape[1]
    h_ref[:, at : at + block] = jnp.zeros((h_ref.shape[0], block), h_ref.dtype)

    def group(g):
        ids, cols, row = unpack(tab, g)
        h = jnp.concatenate([lanes(h_ref, c, block) for c in cols], axis=1)
        w = jnp.concatenate([w_ref[jnp.minimum(s, slots - 1)] for s in ids], axis=1)
        acc[row] += lax.dot_general(
            h, w, (((1,), (1,)), ((), ())), preferred_element_type=jnp.float32
        )

    each(0, total(groups, 0, groups.shape[0]), group, 4)
    panels = panels_of(me[0], 8) if fast else list(range(outs[0].shape[0]))
    for ref in outs:
        for i in range(ref.shape[0]):
            panel = panels.pop(0)
            for j in range(per):
                ref[i, :, j * block : (j + 1) * block] = acc[panel * per + j].astype(ref.dtype)


def grad_kernel(first, shards, heads, cuts, tokens, per, tab, groups, me, count, *refs):
    if first:
        x_in, refs = refs[:shards], refs[shards:]
    else:
        x_ref, sum_ref, refs = refs[0], refs[1], refs[2:]
    n = sum(heads)
    h_in, refs = refs[:n], refs[n:]
    out_ref = refs[0]
    copies = []
    if first:
        x_ref, sems = refs[1:]
        copies = copy_shards(x_in, x_ref, me[0], per, sems)
    slots, part, block = out_ref.shape

    def clear(s, carry):
        out_ref[s] = jnp.zeros((part, block), out_ref.dtype)
        return carry

    lax.fori_loop(jnp.minimum(count[0], slots), slots, clear, 0)
    for copy in copies:
        copy.wait()
    lo = jnp.int32(0)
    for k, head in enumerate(heads):
        mine, h_in = h_in[:head], h_in[head:]
        hi = lo + total(groups, cuts[k], cuts[k + 1])

        def group(g):
            ids, rows, col = unpack(tab, g)
            live = [s < slots for s in ids]
            ids = [jnp.where(l, s, ids[0]) for l, s in zip(live, ids)]
            rows = [jnp.where(l, r, rows[0]) for l, r in zip(live, rows)]
            x = jnp.concatenate([x_ref[r, :, tokens] for r in rows], axis=0)
            h = []
            for ref in mine:
                views = [ref] if len(ref.shape) == 2 else [ref.at[i] for i in range(ref.shape[0])]
                h += [lanes(v, col - cuts[k], block) for v in views]
            h = jnp.concatenate(h, axis=0)
            out = jnp.dot(x, h, preferred_element_type=jnp.float32)
            if not first:
                out += jnp.concatenate([sum_ref[s] for s in ids], axis=0)
            out = out.astype(out_ref.dtype)
            for i, s in enumerate(ids):
                out_ref[s] = out[i * part : (i + 1) * part]

        each(lo, hi, group, 4)
        lo = hi


def quarter_kernel(shards, me, *refs):
    x_in, outs, scratch = refs[:shards], refs[shards:-1], refs[-1]
    block = scratch.shape[1]
    part = outs[0].shape[1]
    per = scratch.shape[0] // shards
    for i, ref in enumerate(x_in):
        for r in range(per):
            scratch[i * per + r] = ref[:, r * block : (r + 1) * block].T
    for j, ref in enumerate(outs):
        at = pl.multiple_of((me[0] ^ j) * part, part)
        ref[...] = scratch[:, pl.ds(at, part), :]


def warm_kernel(w_ref, out_ref, sem):
    copy = pltpu.make_async_copy(w_ref.at[0, 0:8], out_ref, sem)
    copy.start()
    copy.wait()


def join_kernel(*refs):
    refs[-1][...] = jnp.concatenate([ref[...] for ref in refs[:-1]], axis=2)


def along_z(pairs):
    return [(a * 2 + c, b * 2 + c) for a, b in pairs for c in range(2)]


EVEN = along_z([(0, 1), (1, 0), (2, 3), (3, 2)])
ODD = along_z([(1, 2), (2, 1)])
OUTWARD = along_z([(1, 0), (2, 3)])
INWARD = along_z([(0, 1), (3, 2)])
CORES = [(b, b ^ 1) for b in range(8)]
TOK_X = [(t, t ^ 1) for t in range(4)]
TOK_Y = [(t, t ^ 2) for t in range(4)]
TOK_XY = [(t, t ^ 3) for t in range(4)]


def blk(x, pairs):
    return lax.ppermute(x, "blk", pairs)


def tok(x, pairs):
    return lax.ppermute(x, "tok", pairs)


def gather_line(x, middle):
    e1, o1 = blk(x, EVEN), blk(x, ODD)
    p0 = blk(x, CORES)
    o2, e2 = blk(e1, ODD), blk(o1, OUTWARD)
    p1 = blk(e1, CORES)
    e3 = blk(o2, OUTWARD)
    n2 = jnp.where(middle, o1, e2)
    p2 = blk(n2, CORES)
    n3 = jnp.where(middle, o2, e3)
    p3 = blk(n3, CORES)
    return [x, e1, n2, n3, p0, p1, p2, p3]


def call(body, out_shape, in_specs, out_specs, scratch, side=False, **kwargs):
    return pl.pallas_call(
        body,
        out_shape=out_shape,
        in_specs=in_specs,
        out_specs=out_specs,
        scratch_shapes=scratch,
        compiler_params=pltpu.CompilerParams(vmem_limit_bytes=LIMIT, has_side_effects=side),
        **kwargs,
    )


def on_device(n_tok, n_blk, tokens, w_blocks, blk_row, blk_col, blk_count, col_owner, cotangent):
    fast = (n_tok, n_blk) == (4, 8)
    rows_tok, width = tokens.shape
    slots, block, _ = w_blocks.shape
    cols = cotangent.shape[1] // block
    per = width // block
    n_rows = per * n_blk
    part = block // n_tok
    me_blk = lax.axis_index("blk").astype(jnp.int32)
    me_tok = lax.axis_index("tok").astype(jnp.int32)
    z = me_blk // 2
    middle = (z == 1) | (z == 2)
    me = me_blk[None]
    bf16 = tokens.dtype

    def shape(*dims, dtype=bf16):
        return jax.ShapeDtypeStruct(dims, dtype)

    if fast:
        shards = [s[None] for s in gather_line(tokens, middle)]
    else:
        shards = [lax.all_gather(tokens, "blk", axis=0)]

    mine = (col_owner == me_blk)[None, :]
    all_cols = jnp.arange(col_owner.shape[0], dtype=jnp.int32)[None, :]
    local = jnp.sum((mine & (all_cols < blk_col[:, None])).astype(jnp.int32), axis=1)
    live = jnp.arange(slots, dtype=jnp.int32) < blk_count[0]
    col_rank, col_groups = group_ranks(local, live, cols)
    row_rank, row_groups = group_ranks(blk_row, live, n_rows)
    col_tab = group_table(local, blk_row, live, col_rank, col_groups, n_rows)
    row_tab = group_table(blk_row, local, live, row_rank, row_groups, cols)

    def quarter(parts):
        n = len(parts) * per
        return call(
            functools.partial(quarter_kernel, len(parts)),
            [shape(n, part, rows_tok)] * n_tok,
            [SMEM] + [VMEM] * len(parts),
            [VMEM] * n_tok,
            [pltpu.VMEM((n, block, rows_tok), bf16)],
        )(me_tok[None], *parts)

    if fast:
        mine, theirs = [], []
        for k in range(2):
            xq = quarter([s[0] for s in shards[2 * k : 2 * k + 2]])
            xq = [xq[0], tok(xq[1], TOK_X), tok(xq[2], TOK_Y), tok(xq[3], TOK_XY)]
            xq = call(
                join_kernel, shape(2 * per, part, n_tok * rows_tok), [VMEM] * n_tok, VMEM, []
            )(*xq)
            mine.append(xq)
            theirs.append(blk(xq, CORES))
        xq_shards = mine + theirs
    else:
        xq = quarter([tokens])
        order = me_tok ^ jnp.arange(n_tok)
        xq = jnp.take(jnp.stack(xq), order, axis=0)
        xq = lax.all_to_all(xq, "tok", split_axis=0, concat_axis=0, tiled=True)
        xq = xq.transpose(1, 2, 0, 3).reshape(per, part, n_tok * rows_tok)
        xq_shards = [lax.all_gather(xq, "blk", axis=0, tiled=True)]

    call(warm_kernel, shape(8, block), [HBM], VMEM, [pltpu.SemaphoreType.DMA], side=True)(w_blocks)

    cuts = (0, cols // 2, cols)
    hs = []
    x_all = act = None
    for k, (start, stop) in enumerate(zip(cuts[:-1], cuts[1:])):
        n = stop - start
        half = shape(rows_tok, n * block)
        scratch = [pltpu.VMEM((n, rows_tok, block), jnp.float32)]
        if k == 0:
            act, h, x_all = call(
                functools.partial(forward_kernel, len(shards), start, stop),
                [half, half, shape(n_blk + 1, rows_tok, width)],
                [SMEM] * 3 + [ANY] * len(shards) + [VMEM, VMEM],
                [VMEM] * 3,
                scratch + [pltpu.SemaphoreType.DMA((8,))],
            )(col_tab, col_groups, me, *shards, w_blocks, cotangent)
        else:
            act, h = call(
                functools.partial(forward_kernel, 0, start, stop),
                [shape(*cotangent.shape), half],
                [SMEM] * 3 + [VMEM] * 4,
                [HBM, VMEM],
                scratch
                + [pltpu.VMEM((rows_tok, n * block), bf16), pltpu.SemaphoreType.DMA((2,))],
            )(col_tab, col_groups, me, x_all, w_blocks, cotangent, act)
        hs.append(h)

    if fast:
        (a, b) = hs
        ax, ay = tok(a, TOK_X), tok(a, TOK_Y)
        bx, by = tok(b, TOK_X), tok(b, TOK_Y)
        ad, bd = tok(ax, TOK_Y), tok(by, TOK_X)
        near, far = [[a, ax, ay], [b, bx, by]], [[ad], [bd]]
    else:
        near, far = [[lax.all_gather(h, "tok", axis=0)] for h in hs], None

    def term(outs):
        return call(
            functools.partial(term_kernel, len(hs), fast),
            [shape(n, rows_tok, width) for n in outs],
            [SMEM] * 3 + [VMEM] * (len(hs) + 1),
            [VMEM] * len(outs),
            [
                pltpu.VMEM((rows_tok, (cols + 1) * block), bf16),
                pltpu.VMEM((sum(outs) * per, rows_tok, block), jnp.float32),
            ],
        )(row_tab, row_groups, me, *hs, w_blocks)

    def add(*xs):
        return sum(x.astype(jnp.float32) for x in xs).astype(bf16)

    if fast:
        keep, send = term([4, 4])
        q = add(keep, blk(send, CORES))
        own, close, mid, last = (q[i] for i in range(4))
        a1 = blk(last, INWARD)
        b1 = blk(mid, INWARD)
        a2 = blk(add(last, a1), ODD)
        e3 = blk(add(close, a2), EVEN)
        o3 = blk(add(mid, b1), ODD)
        input_grad = add(own, e3, o3)
    else:
        (terms,) = term([n_blk])
        input_grad = lax.psum_scatter(terms, "blk", scatter_dimension=0, tiled=True)[0]

    n_tokens = n_tok * rows_tok
    split = n_tokens - rows_tok if fast else n_tokens
    tables = (col_tab, col_groups, me, blk_count)
    x_shape = (n_rows, part, n_tokens)
    heads = [len(h) for h in near]
    grad, xq_all = call(
        functools.partial(grad_kernel, True, len(xq_shards), heads, cuts, slice(0, split), per),
        [shape(slots, part, block, dtype=jnp.float32 if fast else bf16), shape(*x_shape)],
        [SMEM] * 4 + [ANY] * len(xq_shards) + [VMEM] * sum(heads),
        [VMEM, VMEM],
        [pltpu.SemaphoreType.DMA((8,))],
    )(*tables, *xq_shards, *sum(near, []))
    if fast:
        heads = [len(h) for h in far]
        grad = call(
            functools.partial(grad_kernel, False, 0, heads, cuts, slice(split, n_tokens), per),
            shape(slots, part, block),
            [SMEM] * 4 + [VMEM] * (2 + sum(heads)),
            VMEM,
            [],
        )(*tables, xq_all, grad, *sum(far, []))
    return act, input_grad, grad


def solution(mesh):
    n_tok, n_blk = mesh.shape["tok"], mesh.shape["blk"]

    def body(*args):
        return on_device(n_tok, n_blk, *args)

    return jax.shard_map(
        body,
        mesh=mesh,
        in_specs=(
            P("tok", "blk"),
            P("blk", None, None),
            P("blk"),
            P("blk"),
            P("blk"),
            P(),
            P("tok", "blk"),
        ),
        out_specs=(P("tok", "blk"), P("tok", "blk"), P("blk", "tok", None)),
        check_vma=False,
    )
```

```python
import functools

import jax
import jax.numpy as jnp
from jax import lax
from jax.experimental import pallas as pl
from jax.experimental.pallas import tpu as pltpu
from jax.sharding import PartitionSpec as P


GROUP = 4
UNROLL = (16, 4, 1)
LIMIT = 16 * 1024 * 1024
VMEM = pl.BlockSpec(memory_space=pltpu.VMEM)
SMEM = pl.BlockSpec(memory_space=pltpu.SMEM)
ANY = pl.BlockSpec(memory_space=pl.ANY)
HBM = pl.BlockSpec(memory_space=pltpu.HBM)


def group_ranks(key, live, n_keys):
    ids = jnp.arange(key.shape[0], dtype=jnp.int32)
    keys = jnp.arange(n_keys, dtype=jnp.int32)
    same = (key[:, None] == key[None, :]) & (ids[None, :] < ids[:, None]) & live[None, :]
    rank = jnp.sum(same.astype(jnp.int32), axis=1)
    hit = (key[:, None] == keys[None, :]) & live[:, None]
    return rank, (jnp.sum(hit.astype(jnp.int32), axis=0) + GROUP - 1) // GROUP


def group_table(key, other, live, rank, groups, pad_other):
    slots, n_keys = key.shape[0], groups.shape[0]
    ids = jnp.arange(slots, dtype=jnp.int32)
    keys = jnp.arange(n_keys, dtype=jnp.int32)
    start = jnp.sum(jnp.where(keys[None, :] < key[:, None], groups[None, :], 0), axis=1)
    total = (slots + n_keys * (GROUP - 1) + GROUP - 1) // GROUP * GROUP
    place = jnp.where(live, start * GROUP + rank, total)
    pad = slots | (pad_other << 9)
    entry = ids | (other << 9) | (key << 16)
    at = jnp.arange(total, dtype=jnp.int32)
    return pad + jnp.sum(
        jnp.where(place[None, :] == at[:, None], (entry - pad)[None, :], 0), axis=1
    )


def each(lo, hi, body):
    for unroll in UNROLL:
        n = (hi - lo) // unroll

        def many(i, carry, lo=lo, unroll=unroll):
            for u in range(unroll):
                body(lo + i * unroll + u)
            return carry

        lax.fori_loop(0, n, many, 0)
        lo = lo + n * unroll


def unpack(tab, g):
    entries = [tab[g * GROUP + i] for i in range(GROUP)]
    return (
        [e & 511 for e in entries],
        [lax.shift_right_logical(e, 9) & 127 for e in entries],
        lax.shift_right_logical(entries[0], 16),
    )


def lanes(ref, i, block):
    return ref[:, pl.ds(pl.multiple_of(i * block, block), block)]


def panels_of(me, n):
    if n == 1:
        return [0]
    z, core = lax.shift_right_logical(me, 1), me & 1
    far = [z, z ^ 1, jnp.where(z < 2, 2, 1), jnp.where(z < 2, 3, 0)]
    return [f * 2 + core for f in far] + [f * 2 + 1 - core for f in far]


def total(groups, lo, hi):
    n = jnp.int32(0)
    for i in range(lo, hi):
        n += groups[i]
    return n


def copy_shards(shards, dst, me, per, sems):
    whole = len(shards) == 1
    panels = panels_of(me, 1 if whole else 8)
    copies = []
    for ref in shards:
        n = ref.shape[0] if whole else per
        for i in range(ref.shape[0] // n):
            at = dst.at[pl.ds(panels.pop(0) * per, n)]
            sem = sems.at[len(copies)]
            copies.append(pltpu.make_async_copy(ref.at[pl.ds(i * n, n)], at, sem))
    for copy in copies:
        copy.start()
    return copies


def forward_kernel(shards, start, stop, tab, groups, me, *refs):
    if shards:
        x_in, refs = refs[:shards], refs[shards:]
        w_ref, cot_ref, act_ref, h_ref, x_ref, acc, sems = refs
        copies = copy_shards(x_in, x_ref, me[0], 1, sems)
    else:
        x_ref, w_ref, cot_ref, before, act_out, h_ref, acc, act_ref, sems = refs
        copies = []
    slots, block, _ = w_ref.shape
    per = x_ref.shape[2] // block
    if not shards:
        left = pltpu.make_async_copy(before, act_out.at[:, : start * block], sems.at[0])
        left.start()
    acc[...] = jnp.zeros_like(acc)
    if shards:
        x_ref[x_ref.shape[0] - 1, :, 0:block] = jnp.zeros((x_ref.shape[1], block), x_ref.dtype)
    lo = total(groups, 0, start)
    hi = lo + total(groups, start, stop)
    for copy in copies:
        copy.wait()

    def group(g):
        ids, rows, col = unpack(tab, g)
        x = jnp.concatenate([lanes(x_ref.at[r // per], r % per, block) for r in rows], axis=1)
        w = jnp.concatenate([w_ref[jnp.minimum(s, slots - 1)] for s in ids], axis=0)
        acc[col - start] += jnp.dot(x, w, preferred_element_type=jnp.float32)

    each(lo, hi, group)
    for c in range(stop - start):
        at = slice(c * block, (c + 1) * block)
        hidden = acc[c]
        gate = jax.nn.sigmoid(hidden)
        act_ref[:, at] = (hidden * gate).astype(act_ref.dtype)
        slope = gate * (1.0 + hidden * (1.0 - gate))
        cot = cot_ref[:, (start + c) * block : (start + c + 1) * block]
        h_ref[:, at] = (cot.astype(jnp.float32) * slope).astype(h_ref.dtype)
    if not shards:
        right = pltpu.make_async_copy(
            act_ref, act_out.at[:, start * block : stop * block], sems.at[1]
        )
        right.start()
        left.wait()
        right.wait()


def term_kernel(chunks, fast, tab, groups, me, *refs):
    h_in = refs[:chunks]
    w_ref = refs[chunks]
    outs = refs[chunks + 1 : -2]
    h_ref, acc = refs[-2:]
    slots, block, _ = w_ref.shape
    per = outs[0].shape[2] // block
    acc[...] = jnp.zeros_like(acc)
    at = 0
    for ref in h_in:
        h_ref[:, at : at + ref.shape[1]] = ref[...]
        at += ref.shape[1]
    h_ref[:, at : at + block] = jnp.zeros((h_ref.shape[0], block), h_ref.dtype)

    def group(g):
        ids, cols, row = unpack(tab, g)
        h = jnp.concatenate([lanes(h_ref, c, block) for c in cols], axis=1)
        w = jnp.concatenate([w_ref[jnp.minimum(s, slots - 1)] for s in ids], axis=1)
        acc[row] += lax.dot_general(
            h, w, (((1,), (1,)), ((), ())), preferred_element_type=jnp.float32
        )

    each(0, total(groups, 0, groups.shape[0]), group)
    panels = panels_of(me[0], 8) if fast else list(range(outs[0].shape[0]))
    for ref in outs:
        for i in range(ref.shape[0]):
            panel = panels.pop(0)
            for j in range(per):
                ref[i, :, j * block : (j + 1) * block] = acc[panel * per + j].astype(ref.dtype)


def grad_kernel(first, shards, heads, cuts, tokens, per, tab, groups, me, count, *refs):
    if first:
        x_in, refs = refs[:shards], refs[shards:]
    else:
        x_ref, sum_ref, refs = refs[0], refs[1], refs[2:]
    n = sum(heads)
    h_in, refs = refs[:n], refs[n:]
    out_ref = refs[0]
    copies = []
    if first:
        x_ref, sems = refs[1:]
        copies = copy_shards(x_in, x_ref, me[0], per, sems)
    slots, part, block = out_ref.shape

    def clear(s, carry):
        out_ref[s] = jnp.zeros((part, block), out_ref.dtype)
        return carry

    lax.fori_loop(jnp.minimum(count[0], slots), slots, clear, 0)
    for copy in copies:
        copy.wait()
    lo = jnp.int32(0)
    for k, head in enumerate(heads):
        mine, h_in = h_in[:head], h_in[head:]
        hi = lo + total(groups, cuts[k], cuts[k + 1])

        def group(g):
            ids, rows, col = unpack(tab, g)
            live = [s < slots for s in ids]
            ids = [jnp.where(l, s, ids[0]) for l, s in zip(live, ids)]
            rows = [jnp.where(l, r, rows[0]) for l, r in zip(live, rows)]
            x = jnp.concatenate([x_ref[r, :, tokens] for r in rows], axis=0)
            h = []
            for ref in mine:
                views = [ref] if len(ref.shape) == 2 else [ref.at[i] for i in range(ref.shape[0])]
                h += [lanes(v, col - cuts[k], block) for v in views]
            h = jnp.concatenate(h, axis=0)
            out = jnp.dot(x, h, preferred_element_type=jnp.float32)
            if not first:
                out += jnp.concatenate([sum_ref[s] for s in ids], axis=0)
            out = out.astype(out_ref.dtype)
            for i, s in enumerate(ids):
                out_ref[s] = out[i * part : (i + 1) * part]

        each(lo, hi, group)
        lo = hi


def quarter_kernel(shards, me, *refs):
    x_in, outs, scratch = refs[:shards], refs[shards:-1], refs[-1]
    block = scratch.shape[1]
    part = outs[0].shape[1]
    per = scratch.shape[0] // shards
    for i, ref in enumerate(x_in):
        for r in range(per):
            scratch[i * per + r] = ref[:, r * block : (r + 1) * block].T
    for j, ref in enumerate(outs):
        at = pl.multiple_of((me[0] ^ j) * part, part)
        ref[...] = scratch[:, pl.ds(at, part), :]


def warm_kernel(w_ref, out_ref, sem):
    copy = pltpu.make_async_copy(w_ref.at[0, 0:8], out_ref, sem)
    copy.start()
    copy.wait()


def join_kernel(*refs):
    refs[-1][...] = jnp.concatenate([ref[...] for ref in refs[:-1]], axis=2)


def along_z(pairs):
    return [(a * 2 + c, b * 2 + c) for a, b in pairs for c in range(2)]


EVEN = along_z([(0, 1), (1, 0), (2, 3), (3, 2)])
ODD = along_z([(1, 2), (2, 1)])
OUTWARD = along_z([(1, 0), (2, 3)])
INWARD = along_z([(0, 1), (3, 2)])
CORES = [(b, b ^ 1) for b in range(8)]
TOK_X = [(t, t ^ 1) for t in range(4)]
TOK_Y = [(t, t ^ 2) for t in range(4)]
TOK_XY = [(t, t ^ 3) for t in range(4)]


def blk(x, pairs):
    return lax.ppermute(x, "blk", pairs)


def tok(x, pairs):
    return lax.ppermute(x, "tok", pairs)


def gather_line(x, middle):
    e1, o1 = blk(x, EVEN), blk(x, ODD)
    p0 = blk(x, CORES)
    o2, e2 = blk(e1, ODD), blk(o1, OUTWARD)
    p1 = blk(e1, CORES)
    e3 = blk(o2, OUTWARD)
    n2 = jnp.where(middle, o1, e2)
    p2 = blk(n2, CORES)
    n3 = jnp.where(middle, o2, e3)
    p3 = blk(n3, CORES)
    return [x, e1, n2, n3, p0, p1, p2, p3]


def call(body, out_shape, in_specs, out_specs, scratch, side=False, **kwargs):
    return pl.pallas_call(
        body,
        out_shape=out_shape,
        in_specs=in_specs,
        out_specs=out_specs,
        scratch_shapes=scratch,
        compiler_params=pltpu.CompilerParams(vmem_limit_bytes=LIMIT, has_side_effects=side),
        **kwargs,
    )


def on_device(n_tok, n_blk, tokens, w_blocks, blk_row, blk_col, blk_count, col_owner, cotangent):
    fast = (n_tok, n_blk) == (4, 8)
    rows_tok, width = tokens.shape
    slots, block, _ = w_blocks.shape
    cols = cotangent.shape[1] // block
    per = width // block
    n_rows = per * n_blk
    part = block // n_tok
    me_blk = lax.axis_index("blk").astype(jnp.int32)
    me_tok = lax.axis_index("tok").astype(jnp.int32)
    z = me_blk // 2
    middle = (z == 1) | (z == 2)
    me = me_blk[None]
    bf16 = tokens.dtype

    def shape(*dims, dtype=bf16):
        return jax.ShapeDtypeStruct(dims, dtype)

    if fast:
        shards = [s[None] for s in gather_line(tokens, middle)]
    else:
        shards = [lax.all_gather(tokens, "blk", axis=0)]

    mine = (col_owner == me_blk)[None, :]
    all_cols = jnp.arange(col_owner.shape[0], dtype=jnp.int32)[None, :]
    local = jnp.sum((mine & (all_cols < blk_col[:, None])).astype(jnp.int32), axis=1)
    live = jnp.arange(slots, dtype=jnp.int32) < blk_count[0]
    col_rank, col_groups = group_ranks(local, live, cols)
    row_rank, row_groups = group_ranks(blk_row, live, n_rows)
    col_tab = group_table(local, blk_row, live, col_rank, col_groups, n_rows)
    row_tab = group_table(blk_row, local, live, row_rank, row_groups, cols)

    def quarter(parts):
        n = len(parts) * per
        return call(
            functools.partial(quarter_kernel, len(parts)),
            [shape(n, part, rows_tok)] * n_tok,
            [SMEM] + [VMEM] * len(parts),
            [VMEM] * n_tok,
            [pltpu.VMEM((n, block, rows_tok), bf16)],
        )(me_tok[None], *parts)

    if fast:
        mine, theirs = [], []
        for k in range(2):
            xq = quarter([s[0] for s in shards[2 * k : 2 * k + 2]])
            xq = [xq[0], tok(xq[1], TOK_X), tok(xq[2], TOK_Y), tok(xq[3], TOK_XY)]
            xq = call(
                join_kernel, shape(2 * per, part, n_tok * rows_tok), [VMEM] * n_tok, VMEM, []
            )(*xq)
            mine.append(xq)
            theirs.append(blk(xq, CORES))
        xq_shards = mine + theirs
    else:
        xq = quarter([tokens])
        order = me_tok ^ jnp.arange(n_tok)
        xq = jnp.take(jnp.stack(xq), order, axis=0)
        xq = lax.all_to_all(xq, "tok", split_axis=0, concat_axis=0, tiled=True)
        xq = xq.transpose(1, 2, 0, 3).reshape(per, part, n_tok * rows_tok)
        xq_shards = [lax.all_gather(xq, "blk", axis=0, tiled=True)]

    call(
        warm_kernel, shape(8, block), [HBM], VMEM, [pltpu.SemaphoreType.DMA], side=True
    )(pltpu.with_memory_space_constraint(w_blocks, pltpu.HBM))

    cuts = (0, cols // 2, cols)
    hs = []
    x_all = act = None
    for k, (start, stop) in enumerate(zip(cuts[:-1], cuts[1:])):
        n = stop - start
        half = shape(rows_tok, n * block)
        scratch = [pltpu.VMEM((n, rows_tok, block), jnp.float32)]
        if k == 0:
            act, h, x_all = call(
                functools.partial(forward_kernel, len(shards), start, stop),
                [half, half, shape(n_blk + 1, rows_tok, width)],
                [SMEM] * 3 + [ANY] * len(shards) + [VMEM, VMEM],
                [VMEM] * 3,
                scratch + [pltpu.SemaphoreType.DMA((8,))],
            )(col_tab, col_groups, me, *shards, w_blocks, cotangent)
        else:
            act, h = call(
                functools.partial(forward_kernel, 0, start, stop),
                [shape(*cotangent.shape), half],
                [SMEM] * 3 + [VMEM] * 4,
                [HBM, VMEM],
                scratch
                + [pltpu.VMEM((rows_tok, n * block), bf16), pltpu.SemaphoreType.DMA((2,))],
            )(col_tab, col_groups, me, x_all, w_blocks, cotangent, act)
        hs.append(h)

    if fast:
        (a, b) = hs
        ax, ay = tok(a, TOK_X), tok(a, TOK_Y)
        bx, by = tok(b, TOK_X), tok(b, TOK_Y)
        ad, bd = tok(ay, TOK_X), tok(bx, TOK_Y)
        near, far = [[a, ax, ay], [b, bx, by]], [[ad], [bd]]
    else:
        near, far = [[lax.all_gather(h, "tok", axis=0)] for h in hs], None

    def term(outs):
        return call(
            functools.partial(term_kernel, len(hs), fast),
            [shape(n, rows_tok, width) for n in outs],
            [SMEM] * 3 + [VMEM] * (len(hs) + 1),
            [VMEM] * len(outs),
            [
                pltpu.VMEM((rows_tok, (cols + 1) * block), bf16),
                pltpu.VMEM((sum(outs) * per, rows_tok, block), jnp.float32),
            ],
        )(row_tab, row_groups, me, *hs, w_blocks)

    def add(*xs):
        return sum(x.astype(jnp.float32) for x in xs).astype(bf16)

    if fast:
        keep, send = term([4, 4])
        q = add(keep, blk(send, CORES))
        own, close, mid, last = (q[i] for i in range(4))
        a1 = blk(last, INWARD)
        b1 = blk(mid, INWARD)
        a2 = blk(add(last, a1), ODD)
        e3 = blk(add(close, a2), EVEN)
        o3 = blk(add(mid, b1), ODD)
        input_grad = add(own, e3, o3)
    else:
        (terms,) = term([n_blk])
        input_grad = lax.psum_scatter(terms, "blk", scatter_dimension=0, tiled=True)[0]

    n_tokens = n_tok * rows_tok
    split = n_tokens - rows_tok if fast else n_tokens
    tables = (col_tab, col_groups, me, blk_count)
    x_shape = (n_rows, part, n_tokens)
    heads = [len(h) for h in near]
    grad, xq_all = call(
        functools.partial(grad_kernel, True, len(xq_shards), heads, cuts, slice(0, split), per),
        [shape(slots, part, block, dtype=jnp.float32 if fast else bf16), shape(*x_shape)],
        [SMEM] * 4 + [ANY] * len(xq_shards) + [VMEM] * sum(heads),
        [VMEM, VMEM],
        [pltpu.SemaphoreType.DMA((8,))],
    )(*tables, *xq_shards, *sum(near, []))
    if fast:
        heads = [len(h) for h in far]
        grad = call(
            functools.partial(grad_kernel, False, 0, heads, cuts, slice(split, n_tokens), per),
            shape(slots, part, block),
            [SMEM] * 4 + [VMEM] * (2 + sum(heads)),
            VMEM,
            [],
        )(*tables, xq_all, grad, *sum(far, []))
    return act, input_grad, grad


def solution(mesh):
    n_tok, n_blk = mesh.shape["tok"], mesh.shape["blk"]

    def body(*args):
        return on_device(n_tok, n_blk, *args)

    return jax.shard_map(
        body,
        mesh=mesh,
        in_specs=(
            P("tok", "blk"),
            P("blk", None, None),
            P("blk"),
            P("blk"),
            P("blk"),
            P(),
            P("tok", "blk"),
        ),
        out_specs=(P("tok", "blk"), P("tok", "blk"), P("blk", "tok", None)),
        check_vma=False,
    )
```

```python
import functools

import jax
import jax.numpy as jnp
from jax import lax
from jax.experimental import pallas as pl
from jax.experimental.pallas import tpu as pltpu
from jax.sharding import PartitionSpec as P


GROUP = 4
UNROLL = (16, 4, 1)
LIMIT = 16 * 1024 * 1024
VMEM = pl.BlockSpec(memory_space=pltpu.VMEM)
SMEM = pl.BlockSpec(memory_space=pltpu.SMEM)
ANY = pl.BlockSpec(memory_space=pl.ANY)
HBM = pl.BlockSpec(memory_space=pltpu.HBM)


def group_ranks(key, live, n_keys):
    ids = jnp.arange(key.shape[0], dtype=jnp.int32)
    keys = jnp.arange(n_keys, dtype=jnp.int32)
    same = (key[:, None] == key[None, :]) & (ids[None, :] < ids[:, None]) & live[None, :]
    rank = jnp.sum(same.astype(jnp.int32), axis=1)
    hit = (key[:, None] == keys[None, :]) & live[:, None]
    return rank, (jnp.sum(hit.astype(jnp.int32), axis=0) + GROUP - 1) // GROUP


def group_table(key, other, live, rank, groups, pad_other):
    slots, n_keys = key.shape[0], groups.shape[0]
    ids = jnp.arange(slots, dtype=jnp.int32)
    keys = jnp.arange(n_keys, dtype=jnp.int32)
    start = jnp.sum(jnp.where(keys[None, :] < key[:, None], groups[None, :], 0), axis=1)
    total = (slots + n_keys * (GROUP - 1) + GROUP - 1) // GROUP * GROUP
    place = jnp.where(live, start * GROUP + rank, total)
    pad = slots | (pad_other << 9)
    entry = ids | (other << 9) | (key << 16)
    at = jnp.arange(total, dtype=jnp.int32)
    return pad + jnp.sum(
        jnp.where(place[None, :] == at[:, None], (entry - pad)[None, :], 0), axis=1
    )


def each(lo, hi, body):
    for unroll in UNROLL:
        n = (hi - lo) // unroll

        def many(i, carry, lo=lo, unroll=unroll):
            for u in range(unroll):
                body(lo + i * unroll + u)
            return carry

        lax.fori_loop(0, n, many, 0)
        lo = lo + n * unroll


def unpack(tab, g):
    entries = [tab[g * GROUP + i] for i in range(GROUP)]
    return (
        [e & 511 for e in entries],
        [lax.shift_right_logical(e, 9) & 127 for e in entries],
        lax.shift_right_logical(entries[0], 16),
    )


def lanes(ref, i, block):
    return ref[:, pl.ds(pl.multiple_of(i * block, block), block)]


def panels_of(me, n):
    if n == 1:
        return [0]
    z, core = lax.shift_right_logical(me, 1), me & 1
    far = [z, z ^ 1, jnp.where(z < 2, 2, 1), jnp.where(z < 2, 3, 0)]
    return [f * 2 + core for f in far] + [f * 2 + 1 - core for f in far]


def total(groups, lo, hi):
    n = jnp.int32(0)
    for i in range(lo, hi):
        n += groups[i]
    return n


def copy_shards(shards, dst, me, per, sems):
    whole = len(shards) == 1
    panels = panels_of(me, 1 if whole else 8)
    copies = []
    for ref in shards:
        n = ref.shape[0] if whole else per
        for i in range(ref.shape[0] // n):
            at = dst.at[pl.ds(panels.pop(0) * per, n)]
            sem = sems.at[len(copies)]
            copies.append(pltpu.make_async_copy(ref.at[pl.ds(i * n, n)], at, sem))
    for copy in copies:
        copy.start()
    return copies


def forward_kernel(shards, start, stop, tab, groups, me, *refs):
    if shards:
        x_in, refs = refs[:shards], refs[shards:]
        w_ref, cot_ref, act_ref, h_ref, x_ref, acc, sems = refs
        copies = copy_shards(x_in, x_ref, me[0], 1, sems)
    else:
        x_ref, w_ref, cot_ref, before, act_out, h_ref, acc, act_ref, sems = refs
        copies = []
    slots, block, _ = w_ref.shape
    per = x_ref.shape[2] // block
    if not shards:
        left = pltpu.make_async_copy(before, act_out.at[:, : start * block], sems.at[0])
        left.start()
    acc[...] = jnp.zeros_like(acc)
    if shards:
        x_ref[x_ref.shape[0] - 1, :, 0:block] = jnp.zeros((x_ref.shape[1], block), x_ref.dtype)
    lo = total(groups, 0, start)
    hi = lo + total(groups, start, stop)
    for copy in copies:
        copy.wait()

    def group(g):
        ids, rows, col = unpack(tab, g)
        x = jnp.concatenate([lanes(x_ref.at[r // per], r % per, block) for r in rows], axis=1)
        w = jnp.concatenate([w_ref[jnp.minimum(s, slots - 1)] for s in ids], axis=0)
        acc[col - start] += jnp.dot(x, w, preferred_element_type=jnp.float32)

    each(lo, hi, group)
    for c in range(stop - start):
        at = slice(c * block, (c + 1) * block)
        hidden = acc[c]
        gate = jax.nn.sigmoid(hidden)
        act_ref[:, at] = (hidden * gate).astype(act_ref.dtype)
        slope = gate * (1.0 + hidden * (1.0 - gate))
        cot = cot_ref[:, (start + c) * block : (start + c + 1) * block]
        h_ref[:, at] = (cot.astype(jnp.float32) * slope).astype(h_ref.dtype)
    if not shards:
        right = pltpu.make_async_copy(
            act_ref, act_out.at[:, start * block : stop * block], sems.at[1]
        )
        right.start()
        left.wait()
        right.wait()


def term_kernel(chunks, fast, tab, groups, me, *refs):
    h_in = refs[:chunks]
    w_ref = refs[chunks]
    outs = refs[chunks + 1 : -2]
    h_ref, acc = refs[-2:]
    slots, block, _ = w_ref.shape
    per = outs[0].shape[2] // block
    acc[...] = jnp.zeros_like(acc)
    at = 0
    for ref in h_in:
        h_ref[:, at : at + ref.shape[1]] = ref[...]
        at += ref.shape[1]
    h_ref[:, at : at + block] = jnp.zeros((h_ref.shape[0], block), h_ref.dtype)

    def group(g):
        ids, cols, row = unpack(tab, g)
        h = jnp.concatenate([lanes(h_ref, c, block) for c in cols], axis=1)
        w = jnp.concatenate([w_ref[jnp.minimum(s, slots - 1)] for s in ids], axis=1)
        acc[row] += lax.dot_general(
            h, w, (((1,), (1,)), ((), ())), preferred_element_type=jnp.float32
        )

    each(0, total(groups, 0, groups.shape[0]), group)
    panels = panels_of(me[0], 8) if fast else list(range(outs[0].shape[0]))
    for ref in outs:
        for i in range(ref.shape[0]):
            panel = panels.pop(0)
            for j in range(per):
                ref[i, :, j * block : (j + 1) * block] = acc[panel * per + j].astype(ref.dtype)


def grad_kernel(first, shards, heads, cuts, tokens, per, tab, groups, me, count, *refs):
    if first:
        x_in, refs = refs[:shards], refs[shards:]
    else:
        x_ref, sum_ref, refs = refs[0], refs[1], refs[2:]
    n = sum(heads)
    h_in, refs = refs[:n], refs[n:]
    out_ref = refs[0]
    copies = []
    if first:
        x_ref, sems = refs[1:]
        copies = copy_shards(x_in, x_ref, me[0], per, sems)
    slots, part, block = out_ref.shape

    def clear(s):
        out_ref[s] = jnp.zeros((part, block), out_ref.dtype)

    each(jnp.minimum(count[0], slots), slots, clear)
    for copy in copies:
        copy.wait()
    lo = jnp.int32(0)
    for k, head in enumerate(heads):
        mine, h_in = h_in[:head], h_in[head:]
        hi = lo + total(groups, cuts[k], cuts[k + 1])

        def group(g):
            ids, rows, col = unpack(tab, g)
            live = [s < slots for s in ids]
            ids = [jnp.where(l, s, ids[0]) for l, s in zip(live, ids)]
            rows = [jnp.where(l, r, rows[0]) for l, r in zip(live, rows)]
            x = jnp.concatenate([x_ref[r, :, tokens] for r in rows], axis=0)
            h = []
            for ref in mine:
                views = [ref] if len(ref.shape) == 2 else [ref.at[i] for i in range(ref.shape[0])]
                h += [lanes(v, col - cuts[k], block) for v in views]
            h = jnp.concatenate(h, axis=0)
            out = jnp.dot(x, h, preferred_element_type=jnp.float32)
            if not first:
                out += jnp.concatenate([sum_ref[s] for s in ids], axis=0)
            out = out.astype(out_ref.dtype)
            for i, s in enumerate(ids):
                out_ref[s] = out[i * part : (i + 1) * part]

        each(lo, hi, group)
        lo = hi


def quarter_kernel(shards, me, *refs):
    x_in, outs, scratch = refs[:shards], refs[shards:-1], refs[-1]
    block = scratch.shape[1]
    part = outs[0].shape[1]
    per = scratch.shape[0] // shards
    for i, ref in enumerate(x_in):
        for r in range(per):
            scratch[i * per + r] = ref[:, r * block : (r + 1) * block].T
    for j, ref in enumerate(outs):
        at = pl.multiple_of((me[0] ^ j) * part, part)
        ref[...] = scratch[:, pl.ds(at, part), :]


def warm_kernel(w_ref, out_ref, sem):
    copy = pltpu.make_async_copy(w_ref.at[0, 0:8], out_ref, sem)
    copy.start()
    copy.wait()


def join_kernel(*refs):
    refs[-1][...] = jnp.concatenate([ref[...] for ref in refs[:-1]], axis=2)


def along_z(pairs):
    return [(a * 2 + c, b * 2 + c) for a, b in pairs for c in range(2)]


EVEN = along_z([(0, 1), (1, 0), (2, 3), (3, 2)])
ODD = along_z([(1, 2), (2, 1)])
OUTWARD = along_z([(1, 0), (2, 3)])
INWARD = along_z([(0, 1), (3, 2)])
CORES = [(b, b ^ 1) for b in range(8)]
TOK_X = [(t, t ^ 1) for t in range(4)]
TOK_Y = [(t, t ^ 2) for t in range(4)]
TOK_XY = [(t, t ^ 3) for t in range(4)]


def blk(x, pairs):
    return lax.ppermute(x, "blk", pairs)


def tok(x, pairs):
    return lax.ppermute(x, "tok", pairs)


def gather_line(x, middle):
    e1, o1 = blk(x, EVEN), blk(x, ODD)
    p0 = blk(x, CORES)
    o2, e2 = blk(e1, ODD), blk(o1, OUTWARD)
    p1 = blk(e1, CORES)
    e3 = blk(o2, OUTWARD)
    n2 = jnp.where(middle, o1, e2)
    p2 = blk(n2, CORES)
    n3 = jnp.where(middle, o2, e3)
    p3 = blk(n3, CORES)
    return [x, e1, n2, n3, p0, p1, p2, p3]


def call(body, out_shape, in_specs, out_specs, scratch, side=False, **kwargs):
    return pl.pallas_call(
        body,
        out_shape=out_shape,
        in_specs=in_specs,
        out_specs=out_specs,
        scratch_shapes=scratch,
        compiler_params=pltpu.CompilerParams(vmem_limit_bytes=LIMIT, has_side_effects=side),
        **kwargs,
    )


def on_device(n_tok, n_blk, tokens, w_blocks, blk_row, blk_col, blk_count, col_owner, cotangent):
    fast = (n_tok, n_blk) == (4, 8)
    rows_tok, width = tokens.shape
    slots, block, _ = w_blocks.shape
    cols = cotangent.shape[1] // block
    per = width // block
    n_rows = per * n_blk
    part = block // n_tok
    me_blk = lax.axis_index("blk").astype(jnp.int32)
    me_tok = lax.axis_index("tok").astype(jnp.int32)
    z = me_blk // 2
    middle = (z == 1) | (z == 2)
    me = me_blk[None]
    bf16 = tokens.dtype

    def shape(*dims, dtype=bf16):
        return jax.ShapeDtypeStruct(dims, dtype)

    if fast:
        shards = [s[None] for s in gather_line(tokens, middle)]
    else:
        shards = [lax.all_gather(tokens, "blk", axis=0)]

    mine = (col_owner == me_blk)[None, :]
    all_cols = jnp.arange(col_owner.shape[0], dtype=jnp.int32)[None, :]
    local = jnp.sum((mine & (all_cols < blk_col[:, None])).astype(jnp.int32), axis=1)
    live = jnp.arange(slots, dtype=jnp.int32) < blk_count[0]
    col_rank, col_groups = group_ranks(local, live, cols)
    col_tab = group_table(local, blk_row, live, col_rank, col_groups, n_rows)

    def quarter(parts):
        n = len(parts) * per
        return call(
            functools.partial(quarter_kernel, len(parts)),
            [shape(n, part, rows_tok)] * n_tok,
            [SMEM] + [VMEM] * len(parts),
            [VMEM] * n_tok,
            [pltpu.VMEM((n, block, rows_tok), bf16)],
        )(me_tok[None], *parts)

    if fast:
        mine, theirs = [], []
        for k in range(2):
            xq = quarter([s[0] for s in shards[2 * k : 2 * k + 2]])
            xq = [xq[0], tok(xq[1], TOK_X), tok(xq[2], TOK_Y), tok(xq[3], TOK_XY)]
            xq = call(
                join_kernel, shape(2 * per, part, n_tok * rows_tok), [VMEM] * n_tok, VMEM, []
            )(*xq)
            mine.append(xq)
            theirs.append(blk(xq, CORES))
        xq_shards = mine + theirs
    else:
        xq = quarter([tokens])
        order = me_tok ^ jnp.arange(n_tok)
        xq = jnp.take(jnp.stack(xq), order, axis=0)
        xq = lax.all_to_all(xq, "tok", split_axis=0, concat_axis=0, tiled=True)
        xq = xq.transpose(1, 2, 0, 3).reshape(per, part, n_tok * rows_tok)
        xq_shards = [lax.all_gather(xq, "blk", axis=0, tiled=True)]

    call(
        warm_kernel, shape(8, block), [HBM], VMEM, [pltpu.SemaphoreType.DMA], side=True
    )(pltpu.with_memory_space_constraint(w_blocks, pltpu.HBM))

    cuts = (0, cols // 2, cols)
    hs = []
    x_all = act = None
    for k, (start, stop) in enumerate(zip(cuts[:-1], cuts[1:])):
        n = stop - start
        half = shape(rows_tok, n * block)
        scratch = [pltpu.VMEM((n, rows_tok, block), jnp.float32)]
        if k == 0:
            act, h, x_all = call(
                functools.partial(forward_kernel, len(shards), start, stop),
                [half, half, shape(n_blk + 1, rows_tok, width)],
                [SMEM] * 3 + [ANY] * len(shards) + [VMEM, VMEM],
                [VMEM] * 3,
                scratch + [pltpu.SemaphoreType.DMA((8,))],
            )(col_tab, col_groups, me, *shards, w_blocks, cotangent)
        else:
            act, h = call(
                functools.partial(forward_kernel, 0, start, stop),
                [shape(*cotangent.shape), half],
                [SMEM] * 3 + [VMEM] * 4,
                [HBM, VMEM],
                scratch
                + [pltpu.VMEM((rows_tok, n * block), bf16), pltpu.SemaphoreType.DMA((2,))],
            )(col_tab, col_groups, me, x_all, w_blocks, cotangent, act)
        hs.append(h)

    if fast:
        (a, b) = hs
        ax, ay = tok(a, TOK_X), tok(a, TOK_Y)
        bx, by = tok(b, TOK_X), tok(b, TOK_Y)
        ad, bd = tok(ay, TOK_X), tok(bx, TOK_Y)
        near, far = [[a, ax, ay], [b, bx, by]], [[ad], [bd]]
    else:
        near, far = [[lax.all_gather(h, "tok", axis=0)] for h in hs], None

    rows_late, hs[0] = lax.optimization_barrier((blk_row, hs[0]))
    row_rank, row_groups = group_ranks(rows_late, live, n_rows)
    row_tab = group_table(rows_late, local, live, row_rank, row_groups, cols)

    def term(outs):
        return call(
            functools.partial(term_kernel, len(hs), fast),
            [shape(n, rows_tok, width) for n in outs],
            [SMEM] * 3 + [VMEM] * (len(hs) + 1),
            [VMEM] * len(outs),
            [
                pltpu.VMEM((rows_tok, (cols + 1) * block), bf16),
                pltpu.VMEM((sum(outs) * per, rows_tok, block), jnp.float32),
            ],
        )(row_tab, row_groups, me, *hs, w_blocks)

    def add(*xs):
        return sum(x.astype(jnp.float32) for x in xs).astype(bf16)

    if fast:
        keep, send = term([4, 4])
        q = add(keep, blk(send, CORES))
        own, close, mid, last = (q[i] for i in range(4))
        a1 = blk(last, INWARD)
        b1 = blk(mid, INWARD)
        a2 = blk(add(last, a1), ODD)
        e3 = blk(add(close, a2), EVEN)
        o3 = blk(add(mid, b1), ODD)
        input_grad = add(own, e3, o3)
    else:
        (terms,) = term([n_blk])
        input_grad = lax.psum_scatter(terms, "blk", scatter_dimension=0, tiled=True)[0]

    n_tokens = n_tok * rows_tok
    split = n_tokens - rows_tok if fast else n_tokens
    tables = (col_tab, col_groups, me, blk_count)
    x_shape = (n_rows, part, n_tokens)
    heads = [len(h) for h in near]
    grad, xq_all = call(
        functools.partial(grad_kernel, True, len(xq_shards), heads, cuts, slice(0, split), per),
        [shape(slots, part, block, dtype=jnp.float32 if fast else bf16), shape(*x_shape)],
        [SMEM] * 4 + [ANY] * len(xq_shards) + [VMEM] * sum(heads),
        [VMEM, VMEM],
        [pltpu.SemaphoreType.DMA((8,))],
    )(*tables, *xq_shards, *sum(near, []))
    if fast:
        heads = [len(h) for h in far]
        grad = call(
            functools.partial(grad_kernel, False, 0, heads, cuts, slice(split, n_tokens), per),
            shape(slots, part, block),
            [SMEM] * 4 + [VMEM] * (2 + sum(heads)),
            VMEM,
            [],
        )(*tables, xq_all, grad, *sum(far, []))
    return act, input_grad, grad


def solution(mesh):
    n_tok, n_blk = mesh.shape["tok"], mesh.shape["blk"]

    def body(*args):
        return on_device(n_tok, n_blk, *args)

    return jax.shard_map(
        body,
        mesh=mesh,
        in_specs=(
            P("tok", "blk"),
            P("blk", None, None),
            P("blk"),
            P("blk"),
            P("blk"),
            P(),
            P("tok", "blk"),
        ),
        out_specs=(P("tok", "blk"), P("tok", "blk"), P("blk", "tok", None)),
        check_vma=False,
    )
```
